32 devices in a mesh: row: 4 (over z), col: 8 (over y, x, core).
Axes of the slice: x: 2, y: 2, z: 4, core: 2. Of those that a mesh axis runs over, the one named last changes fastest.
Arguments:
- strain: bfloat16 [256, 33280], P(('row', 'col')), may hold values from -6 to 6
- file_channels: int32 [256], P(('row', 'col')), may hold values from 0 to 127, as said below
- file_counts: int32 [32], P(('row', 'col')), may hold values from 0 to 8, as said below
- window_start: int32 [32], P(('row', 'col')), may hold values from 0 to 512
Outputs:
- correlations: bfloat16 [128, 128, 1024], P('row', 'col')
The draws below stay inside these ranges and needn't reach their ends.
Inputs may be any that keep to these rules, and one draw needn't show every extreme that they name: `file_channels`: the first file_counts[d] slots of file d are live. The live slots of the 4 files with one col index hold, each exactly once, the channels g whose owner ((g // 4) // 8, (g // 4) % 8) has that col index; dead slots hold arbitrary channel numbers. One file holds at most 2 channels of one owner, and exactly 2 for some file and owner in every group of files with one col index. `file_counts`: in every group of files with one col index some file has all 8 slots live.
All inputs are finite; a program needn't handle non-finite values.
Results may differ from the reference program's by a relative error of at most 0.0076.
Values may be sent and summed in bfloat16 or wider, within the bound.
A program may use at most 128 MiB of HBM per device.

```python
import math
import jax
import jax.numpy as jnp
from jax import lax

NF = 2048
NT = 4096
LAGS = 1024
SEGS = 8
CH_DEV = 4
CAP = 2
SPAN = 512
SMOOTH = 32
EDGE = 128
SLOTS = 8
NCH = 128
TFILE = 33280
N_ROW = 4
N_COL = 8
DEVICES = 32


def file_layout(key):
    layout_key = jax.random.fold_in(key, 11)
    column_keys = jax.random.split(layout_key, N_COL)

    def one_column(column_key, column):
        sub_keys = jax.random.split(column_key, 5)
        file_order = jax.random.permutation(sub_keys[0], N_ROW)
        offsets = jax.random.randint(sub_keys[2], (N_ROW,), 0, N_ROW - 1)
        owners = jnp.repeat(jnp.arange(N_ROW, dtype=jnp.int32), CH_DEV)
        within = jnp.tile(jnp.arange(CH_DEV, dtype=jnp.int32), N_ROW)
        hot_pair = within < CAP
        spread = within - CAP
        position = jnp.where(hot_pair, 0, 1 + jnp.mod(offsets[owners] + spread, N_ROW - 1))
        file_of = file_order[position].astype(jnp.int32)
        channels = ((owners * N_COL + column) * CH_DEV + within).astype(jnp.int32)
        item_count = N_ROW * CH_DEV
        ranking = jax.random.permutation(sub_keys[3], item_count).astype(jnp.int32)
        sorted_index = jnp.argsort(file_of * item_count + ranking, stable=True)
        sorted_files = file_of[sorted_index]
        counts = jnp.sum((file_of[None, :] == jnp.arange(N_ROW, dtype=jnp.int32)[:, None]).astype(jnp.int32), axis=1)
        starts = jnp.cumsum(counts) - counts
        slot_of = jnp.arange(item_count, dtype=jnp.int32) - starts[sorted_files]
        filler = jax.random.randint(sub_keys[4], (N_ROW, SLOTS), 0, NCH)
        slot_table = filler.at[sorted_files, slot_of].set(channels[sorted_index])
        return (slot_table.astype(jnp.int32), counts.astype(jnp.int32))
    tables, counts = jax.vmap(one_column)(column_keys, jnp.arange(N_COL, dtype=jnp.int32))
    return (jnp.transpose(tables, (1, 0, 2)).reshape(-1), jnp.transpose(counts).reshape(-1))


def draw_file_channels(key, part):
    return file_layout(key)[0]


def draw_file_counts(key, part):
    return file_layout(key)[1]


def touch_ends(drawn, own_key, least, high):
    place = [jax.random.randint(jax.random.fold_in(own_key, axis), (), 0, length) for axis, length in enumerate(drawn.shape)]
    main_axis = drawn.shape.index(max(drawn.shape))
    neighbour = place[:main_axis] + [(place[main_axis] + 1) % drawn.shape[main_axis]] + place[main_axis + 1:]
    return drawn.at[tuple(place)].set(least).at[tuple(neighbour)].set(high)


def level_of(key, dims, pieces, smallest, largest):
    loudness, own = 1.0, jax.random.fold_in(key, 6)
    for dim, shards_of in pieces:
        draws = jnp.exp(jax.random.uniform(jax.random.fold_in(own, dim), (shards_of,), jnp.float32, smallest / len(pieces), largest / len(pieces)))
        loudness = loudness * jnp.repeat(draws, dims[dim] // shards_of).reshape([-1 if axis == dim else 1 for axis in range(len(dims))])
    return loudness


def bell_draw(key, shape, scale, bound, shards=(), kind=jnp.bfloat16):
    values = jax.random.normal(key, shape, jnp.float32) * scale
    if len(shards) > 0:
        values = level_of(key, shape, shards, -0.22, 0.18) * values
    return jnp.clip(values, min=-bound, max=bound).astype(kind)


def setup_inputs(seed: int = 0) -> dict:
    key_list = jax.random.split(jax.random.key(seed), 5)
    strain = bell_draw(key_list[0], (DEVICES * SLOTS, TFILE), 1.0, 6.0, ((0, 32),))
    file_channels = draw_file_channels(jax.random.fold_in(key_list[4], 71), 0)
    file_counts = draw_file_counts(jax.random.fold_in(key_list[4], 71), 0)
    window_start = touch_ends(jax.random.randint(key_list[3], (DEVICES,), 0, SPAN + 1), jax.random.fold_in(key_list[3], 1), 0, SPAN).astype(jnp.int32)
    return {"strain": strain, "file_channels": file_channels, "file_counts": file_counts, "window_start": window_start}


def dft_block(first_freq, freq_count, length):
    sample_index = jnp.arange(length, dtype=jnp.int32)[:, None]
    freq_index = first_freq + jnp.arange(freq_count, dtype=jnp.int32)[None, :]
    phases = jnp.mod(sample_index * freq_index, length).astype(jnp.float32) * (2.0 * math.pi / length)
    return jnp.concatenate([jnp.cos(phases), -jnp.sin(phases)], axis=1).astype(jnp.bfloat16)

def lag_table():
    freq_index = jnp.arange(NF, dtype=jnp.int32)[:, None]
    lag_index = jnp.arange(LAGS, dtype=jnp.int32)[None, :] - LAGS // 2
    phases = jnp.mod(freq_index * lag_index, NT).astype(jnp.float32) * (2.0 * math.pi / NT)
    return jnp.concatenate([jnp.cos(phases), -jnp.sin(phases)], axis=0).astype(jnp.bfloat16)

def band_taper(freq_count):
    freq_index = jnp.arange(freq_count, dtype=jnp.float32)
    distance = jnp.minimum(freq_index + 0.5, freq_count - freq_index - 0.5)
    rising = jnp.minimum(distance / EDGE, 1.0)
    return jnp.sin(0.5 * math.pi * rising) ** 2

def whiten(real_part, imag_part):
    powers = real_part * real_part + imag_part * imag_part
    padded = jnp.pad(powers, ((0, 0), (SMOOTH + 1, SMOOTH)))
    running = jnp.cumsum(padded, axis=1)
    window_sum = running[:, 2 * SMOOTH + 1:] - running[:, :powers.shape[1]]
    scaling = band_taper(powers.shape[1])[None, :] / jnp.sqrt(window_sum / (2 * SMOOTH + 1) + 1e-06)
    return (real_part * scaling, imag_part * scaling)

def reference(strain, file_channels, file_counts, window_start):
    file_total = file_counts.shape[0]
    file_blocks = strain.reshape(file_total, SLOTS, strain.shape[1])

    def cut_window(block, first_sample):
        return lax.dynamic_slice_in_dim(block, first_sample, SEGS * NT, 1)
    windows = jax.vmap(cut_window)(file_blocks, window_start).reshape(file_total * SLOTS, SEGS * NT)
    live_slot = (jnp.arange(SLOTS, dtype=jnp.int32)[None, :] < file_counts[:, None]).reshape(-1)
    target = jnp.where(live_slot, file_channels, NCH).astype(jnp.int32)
    traces = jnp.zeros((NCH + 1, SEGS * NT), jnp.bfloat16).at[target].set(windows)[:NCH]
    segment_rows = traces.reshape(NCH * SEGS, NT).astype(jnp.float32)
    table = dft_block(jnp.int32(0), NF, NT).astype(jnp.float32)
    product = jnp.dot(segment_rows, table, precision=lax.Precision.HIGHEST)
    real_part, imag_part = whiten(product[:, :NF], product[:, NF:])
    spectra = jnp.stack([real_part.reshape(NCH, SEGS, NF), imag_part.reshape(NCH, SEGS, NF)], axis=1).astype(jnp.bfloat16)
    spectra = lax.optimization_barrier(spectra).astype(jnp.float32)
    column = jnp.arange(NCH, dtype=jnp.int32)
    group_size = N_ROW * CH_DEV
    col_ids = (column % group_size // CH_DEV * N_COL + column // group_size) * CH_DEV + column % CH_DEV
    col_spectra = spectra[col_ids]
    flipped = jnp.concatenate([-col_spectra[:, 1:2], col_spectra[:, 0:1]], axis=1)
    inverse = lag_table().astype(jnp.float32)
    norm_scale = 1.0 / math.sqrt(SEGS * NF)

    def one_block(block_index):
        first_row = block_index * 8
        row_block = lax.dynamic_slice_in_dim(spectra, first_row, 8, 0)
        real_cross = jnp.einsum('icsf,jcsf->ijf', row_block, col_spectra, precision=lax.Precision.HIGHEST)
        imag_cross = jnp.einsum('icsf,jcsf->ijf', row_block, flipped, precision=lax.Precision.HIGHEST)
        cross = jnp.concatenate([real_cross, imag_cross], axis=2).astype(jnp.bfloat16)
        cross = lax.optimization_barrier(cross).astype(jnp.float32)
        lagged = jnp.dot(cross.reshape(8 * NCH, 2 * NF), inverse, precision=lax.Precision.HIGHEST).reshape(8, NCH, LAGS)
        row_ids = first_row + jnp.arange(8, dtype=jnp.int32)
        keep_pair = (row_ids[:, None] != col_ids[None, :]).astype(jnp.float32)
        return (lagged * (keep_pair[:, :, None] * norm_scale)).astype(jnp.bfloat16)
    blocks_out = lax.map(one_block, jnp.arange(NCH // 8, dtype=jnp.int32))
    return blocks_out.reshape(NCH, NCH, LAGS)
```

```python
import functools
import math

import jax
import jax.numpy as jnp
import numpy as np
from jax import lax
from jax.experimental import pallas as pl
from jax.experimental.pallas import tpu as pltpu
from jax.sharding import PartitionSpec as P

NF = 2048
NT = 4096
LAGS = 1024
SEGS = 8
CH_DEV = 4
CAP = 2
SMOOTH = 32
EDGE = 128
N1 = 16
N2 = NT // N1
F2 = NF // N1
HALF = LAGS // 2
PARTS = 2
PSEG = SEGS // PARTS
ROWS = CH_DEV * PSEG
BLOCK = 2 * ROWS
QUADS = 4
PAIR = QUADS * F2
TURNS = NF // PAIR
STEPS = PARTS * TURNS
TILE = 256
TILES = 2 * HALF // TILE
CORES = 2
AHEAD = 4
MESH = pl.DeviceIdType.MESH


def forward_tables():
    n2 = np.arange(N2)
    f1 = np.arange(N1)
    f2 = np.arange(F2)
    angle = 2 * np.pi * (np.outer(f1, n2) % NT) / NT
    twiddle = np.stack([np.cos(angle), -np.sin(angle)]).astype(np.float32)
    angle = 2 * np.pi * (np.outer(n2, f2) % N2) / N2
    c, s = np.cos(angle), np.sin(angle)
    second = np.block([[c, -s], [s, c]]).astype(np.float32)
    high = second.astype(jnp.bfloat16)
    low = (second - high.astype(np.float32)).astype(jnp.bfloat16)
    f = f1[:, None] + N1 * f2[None, :]
    distance = np.minimum(f + 0.5, NF - f - 0.5)
    taper = np.sin(0.5 * np.pi * np.minimum(distance / EDGE, 1.0)) ** 2
    turn = np.pi * f / NT
    shape = np.stack([taper, np.cos(turn), -np.sin(turn)]).astype(np.float32)
    return twiddle, high, low, shape


def lag_tables():
    m2 = 2 * np.arange(HALF) + 1
    f1 = np.arange(N1)
    f2 = N1 * np.arange(F2)
    a = np.pi * (np.outer(f1, m2) % (2 * NT)) / NT
    b = np.pi * (np.outer(f2, m2) % (2 * NT)) / NT
    first = np.stack([np.cos(a), np.sin(a)]).astype(np.float32)
    second = np.stack([np.cos(b), np.sin(b)]).astype(np.float32)
    return first, second


def shifted(value, lanes, amount):
    rolled = pltpu.roll(value, amount % F2, 1)
    source = lanes - amount
    return jnp.where((source >= 0) & (source < F2), rolled, 0.0)


def greet(axes):
    barrier = pltpu.get_barrier_semaphore()
    count = 0
    for axis in axes:
        size, me = lax.axis_size(axis), lax.axis_index(axis)
        for d in range(1, size):
            pl.semaphore_signal(barrier, inc=1, device_id={axis: lax.rem(me + d, size)}, device_id_type=MESH)
            count += 1
    pl.semaphore_wait(barrier, count)


def tree(terms):
    while len(terms) > 1:
        terms = [terms[k] + terms[k + 1] for k in range(0, len(terms), 2)]
    return terms[0]


def combine(values, weights):
    total = None
    for v, w in zip(values, weights):
        if abs(w) < 1e-9:
            continue
        term = v if abs(w - 1) < 1e-9 else (-v if abs(w + 1) < 1e-9 else v * np.float32(w))
        total = term if total is None else total + term
    return total


def dot(a, b):
    return jnp.dot(a, b, preferred_element_type=jnp.float32)


def chosen_rows(label):
    count = label.shape[0]
    row = lax.broadcasted_iota(jnp.int32, label.shape, 0)
    lane = lax.broadcasted_iota(jnp.int32, label.shape, 1)
    hit = (label == (lane // PSEG).astype(jnp.float32)) & (lax.rem(row, PSEG) == lax.rem(lane, PSEG))
    picks = jnp.where(hit, 1.0, 0.0)
    if count < 128:
        picks = jnp.concatenate([picks, jnp.zeros((128 - count, 128), jnp.float32)], axis=0)
    return jnp.transpose(picks)[:ROWS, :count].astype(jnp.bfloat16)


def spectra_part(part, picks, got, x_ref, z_ref, tw_ref, hi_ref, lo_ref, shape_ref, put):
    x_ref[...] = dot(picks, got[part].reshape(-1, NT))
    cosines = np.cos(2 * np.pi * np.arange(N1) / N1)
    sines = np.sin(2 * np.pi * np.arange(N1) / N1)
    for h in range(0, N2, 128):
        xs = [x_ref[:, k * N2 + h : k * N2 + h + 128] for k in range(N1)]
        even = [xs[k] + xs[k + N1 // 2] for k in range(N1 // 2)]
        odd = [xs[k] - xs[k + N1 // 2] for k in range(N1 // 2)]
        for f in range(N1 // 2 + 1):
            src = even if f % 2 == 0 else odd
            re = combine(src, [cosines[f * k % N1] for k in range(N1 // 2)])
            im = combine(src, [-sines[f * k % N1] for k in range(N1 // 2)])
            for f1, sign in {f: 1.0, (N1 - f) % N1: -1.0}.items() if f not in (0, N1 // 2) else ((f, 1.0),):
                tc = tw_ref[0, f1 : f1 + 1, h : h + 128]
                ts = tw_ref[1, f1 : f1 + 1, h : h + 128]
                if im is None:
                    zr, zi = re * tc, re * ts
                else:
                    i = im if sign > 0 else -im
                    zr, zi = re * tc - i * ts, re * ts + i * tc
                z_ref[f1 * ROWS : (f1 + 1) * ROWS, h : h + 128] = zr
                z_ref[f1 * ROWS : (f1 + 1) * ROWS, N2 + h : N2 + h + 128] = zi
    z = z_ref[...]
    zh = z.astype(jnp.bfloat16)
    zl = (z - zh.astype(jnp.float32)).astype(jnp.bfloat16)
    z_ref[:, : 2 * F2] = dot(zh, hi_ref[...]) + dot(zl, hi_ref[...]) + dot(zh, lo_ref[...])
    lanes = lax.broadcasted_iota(jnp.int32, (ROWS, F2), 1)
    piece = lambda f1, c: z_ref[f1 * ROWS : (f1 + 1) * ROWS, c * F2 : (c + 1) * F2]
    power = []
    for f1 in range(N1):
        re, im = piece(f1, 0), piece(f1, 1)
        power.append(re * re + im * im)
    prefix, suffix = [power[0]], [power[-1]]
    for k in range(1, N1):
        prefix.append(prefix[-1] + power[k])
        suffix.append(suffix[-1] + power[N1 - 1 - k])
    suffix = suffix[::-1]
    total = prefix[-1]
    reach = SMOOTH // N1
    middle = total
    for k in range(1, reach):
        middle = middle + shifted(total, lanes, k) + shifted(total, lanes, -k)
    for f1 in range(N1):
        window = middle + shifted(suffix[f1], lanes, reach) + shifted(prefix[f1], lanes, -reach)
        scale = shape_ref[0, f1 : f1 + 1] * lax.rsqrt(window * (1.0 / (2 * SMOOTH + 1)) + 1e-06)
        re, im = piece(f1, 0) * scale, piece(f1, 1) * scale
        tc, ts = shape_ref[1, f1 : f1 + 1], shape_ref[2, f1 : f1 + 1]
        put(part * TURNS + f1 // QUADS, f1 % QUADS, re, im, re * tc - im * ts, re * ts + im * tc)


def pair_kernel(out_ref, lab_ref, *refs):
    sources, refs = refs[:8], refs[8:]
    result, consts, refs = refs[0], refs[1:9], refs[9:]
    tw_ref, hi_ref, lo_ref, shape_ref, first_ref, second_ref, perm_ref, flip_ref = consts
    got, glab, x_ref, z_ref, w_ref, row_all, col_all, v_ref, b32, cross, acc, down_ref = refs[:12]
    a_send, a_recv, lab_recv, z_send, z_far, z_rest, x_send, x_same, x_mate, const_sem = refs[12:]
    rows, cols = lax.axis_size("row"), lax.axis_size("col")
    row_total, col_total = cols * CH_DEV, rows * CH_DEV
    share = col_total // TILES
    row_me, col_me = lax.axis_index("row"), lax.axis_index("col")
    hops, chips = rows // 2, cols // CORES
    far = lax.rem(row_me + hops, rows)
    chip, core = col_me // CORES, lax.rem(col_me, CORES)
    mate = chip * CORES + (1 - core)
    chip_at = lambda d: lax.rem(chip + chips - d, chips) * CORES

    loads = [pltpu.make_async_copy(f, t, const_sem.at[k]) for k, (f, t) in enumerate(zip(sources, consts))]
    for load in loads[::-1]:
        load.start()
    greet(("row", "col"))

    def remote(src, dst, send, recv, peer):
        return pltpu.make_async_remote_copy(
            src_ref=src, dst_ref=dst, send_sem=send, recv_sem=recv, device_id=peer, device_id_type=MESH
        )

    def settle(ref, sem):
        pltpu.make_async_copy(ref, ref, sem).wait()

    for d in range(1, rows):
        peer = lax.rem(row_me + d, rows)
        remote(lab_ref.at[peer], glab.at[d], a_send.at[PARTS], lab_recv, {"row": peer}).start()
    for part in range(PARTS):
        for d in range(1, rows):
            peer = lax.rem(row_me + d, rows)
            remote(out_ref.at[part, peer], got.at[part, d], a_send.at[part], a_recv.at[part], {"row": peer}).start()
    glab[0] = lab_ref[row_me]
    for part in range(PARTS):
        got[part, 0] = out_ref[part, row_me]

    def z_copy(u, origin, peer, k):
        sem = z_far if k < 2 else z_rest
        return remote(col_all.at[u, origin], col_all.at[u, origin], z_send.at[k], sem.at[u], {"row": peer})

    def x_copy(u, origin, peer, k):
        sem = x_same if k == 0 else x_mate
        return remote(row_all.at[u, origin], row_all.at[u, origin], x_send.at[k], sem.at[u], {"col": peer})

    def z_plans(u):
        out = []
        for d in range(1, hops + 1):
            up, down = row_me + d, row_me - d
            k = 0 if d == hops else 2 * d
            out.append((up < rows, z_copy(u, row_me, up, k)))
            out.append((down >= 0, z_copy(u, row_me, down, k + 1)))
        return out

    def relay_plans(u):
        out = []
        for d in range(1, hops):
            up, down = row_me + d, row_me - d
            k = 2 * hops + d - 1
            out.append(((far < row_me) & (up < rows), z_copy(u, far, up, k)))
            out.append(((far > row_me) & (down >= 0), z_copy(u, far, down, k)))
        return out

    def begin_z(u):
        for valid, copy in z_plans(u):
            pl.when(valid)(copy.start)

    def begin_x(u):
        for d in range(1, chips):
            x_copy(u, col_me, chip_at(d) + core, 0).start()
        x_copy(u, col_me, mate, 1).start()

    def serve(u):
        settle(col_all.at[u, pl.ds(0, 1)], z_far.at[u])
        for valid, copy in relay_plans(u):
            pl.when(valid)(copy.start)
        settle(row_all.at[u, pl.ds(0, chips - 1)], x_same.at[u])
        for d in range(1, chips):
            x_copy(u, chip_at(d) + core, mate, 2).start()

    def arrive(u):
        settle(col_all.at[u, pl.ds(0, rows - 2)], z_rest.at[u])
        settle(row_all.at[u, pl.ds(0, chips)], x_mate.at[u])
        for q in range(0, QUADS, 2):
            sides = [row_all[u, :, q + n].reshape(-1, F2) for n in range(2)]
            turned = dot(perm_ref[...], jnp.concatenate(sides, axis=1)).astype(jnp.bfloat16)
            for n in range(2):
                for k in range(2 * PSEG):
                    v_ref[q + n, k] = turned[k * row_total : (k + 1) * row_total, n * F2 : (n + 1) * F2]
        for q in range(QUADS):
            b32[q] = col_all[u, :, q].reshape(b32.shape[1:]).astype(jnp.float32)

    def put(u, q, re, im, tr, ti):
        for c, (a, b) in enumerate(((re, tr), (im, ti))):
            at = slice(c * ROWS, (c + 1) * ROWS)
            col_all[u, row_me, q, at] = a.astype(jnp.bfloat16)
            row_all[u, col_me, q, at] = b.astype(jnp.bfloat16)

    def cross_rows(i, now):
        for jj in range(share):
            base = pl.multiple_of((i * (share // CH_DEV) + jj // CH_DEV) * BLOCK, BLOCK)
            at = base + jj % CH_DEV * PSEG
            for q in range(QUADS):
                spread = lambda r: jnp.broadcast_to(b32[q, pl.ds(at + r, 1), :], (16, F2)).astype(jnp.bfloat16)
                br = [spread(s) for s in range(PSEG)]
                bi = [spread(ROWS + s) for s in range(PSEG)]
                for g in range(0, row_total, 16):
                    real, imag = [], []
                    for s in range(PSEG):
                        ar, ai = v_ref[q, s, g : g + 16], v_ref[q, PSEG + s, g : g + 16]
                        real.append(ar * br[s] + ai * bi[s])
                        imag.append(ai * br[s] - ar * bi[s])
                    line = pl.ds(pl.multiple_of((i * share + jj) * row_total + g, 16), 16)
                    cross[now, 0, q, line] = tree(real)
                    cross[now, 1, q, line] = tree(imag)

    def lag_tile(i, u):
        before = lax.rem(u + 1, 2)
        side = [cross[before, i // (TILES // 2), q] for q in range(QUADS)]
        term = dot(jnp.concatenate(side, axis=1), w_ref[lax.rem(u - 1, TURNS), i])
        for n in range(2):
            acc[i, n] = acc[i, n] + term[:, n * F2 : (n + 1) * F2]

    for load in loads:
        load.wait()
    for k in range(HALF // TILE):
        lane = slice(k * TILE, (k + 1) * TILE)
        bc, bs = second_ref[0, :, lane], second_ref[1, :, lane]
        for f1 in range(N1):
            ac, as_ = first_ref[0, f1 : f1 + 1, lane], first_ref[1, f1 : f1 + 1, lane]
            t, at = f1 * F2 // PAIR, slice(f1 * F2 % PAIR, f1 * F2 % PAIR + F2)
            w_ref[t, k, at, :] = (ac * bc - as_ * bs).astype(jnp.bfloat16)
            w_ref[t, HALF // TILE + k, at, :] = (-(as_ * bc + ac * bs)).astype(jnp.bfloat16)
    acc[...] = jnp.zeros_like(acc)

    tables = (tw_ref, hi_ref, lo_ref, shape_ref)
    settle(glab.at[pl.ds(1, rows - 1)], lab_recv)
    settle(got.at[0, pl.ds(1, rows - 1)], a_recv.at[0])
    picks = chosen_rows(glab[...].reshape(-1, 128).astype(jnp.float32))
    spectra_part(0, picks, got, x_ref, z_ref, *tables, put)

    @pl.loop(0, TURNS)
    def _(u):
        begin_z(u)
        begin_x(u)

    serve(0)
    settle(got.at[1, pl.ds(1, rows - 1)], a_recv.at[1])
    spectra_part(1, picks, got, x_ref, z_ref, *tables, put)

    @pl.loop(TURNS, STEPS)
    def _(u):
        begin_z(u)
        begin_x(u)

    arrive(0)

    @pl.loop(0, TILES)
    def _(i):
        cross_rows(i, 0)

        @pl.when(i == 1)
        def _():
            serve(1)

    @pl.loop(1, STEPS)
    def _(u):
        arrive(u)

        @pl.loop(0, TILES)
        def _(i):
            lag_tile(i, u)
            cross_rows(i, lax.rem(u, 2))

            @pl.when((i == 1) & (u + 1 < STEPS))
            def _():
                serve(u + 1)

    @pl.loop(0, TILES)
    def _(i):
        lag_tile(i, STEPS)

    half = TILES // 2
    place = lax.broadcasted_iota(jnp.int32, (col_total, F2), 0)
    scale = np.float32(1.0 / math.sqrt(SEGS * NF))

    @pl.loop(0, row_total)
    def _(g):
        own = g - col_me * CH_DEV
        mine = (place == row_me * CH_DEV + own) & (own >= 0) & (own < CH_DEV)
        keep = jnp.where(mine, 0.0, scale)
        for k in range(half):
            for n in range(2):
                a = acc[k, n, pl.ds(g, col_total, stride=row_total), :]
                b = acc[half + k, n, pl.ds(g, col_total, stride=row_total), :]
                first = HALF + k * TILE + n * F2
                result[g, :, first : first + F2] = ((a + b) * keep).astype(jnp.bfloat16)
                down_ref[k, n, pl.ds(pl.multiple_of(g * col_total, 16), col_total), :] = ((a - b) * keep).astype(jnp.bfloat16)

    for k in range(half):
        side = jnp.concatenate([down_ref[k, n] for n in range(2)], axis=1)
        turned = dot(side, flip_ref[...]).astype(jnp.bfloat16)
        result[:, :, HALF - (k + 1) * TILE : HALF - k * TILE] = turned.reshape(row_total, col_total, TILE)

    settle(glab.at[pl.ds(1, rows - 1)], a_send.at[PARTS])
    for part in range(PARTS):
        settle(got.at[part, pl.ds(1, rows - 1)], a_send.at[part])
    for d in range(1, hops + 1):
        k = 0 if d == hops else 2 * d
        pl.when(row_me + d < rows)(lambda k=k: settle(col_all.at[:, 0], z_send.at[k]))
        pl.when(row_me - d >= 0)(lambda k=k: settle(col_all.at[:, 0], z_send.at[k + 1]))
    for d in range(1, hops):
        k = 2 * hops + d - 1
        valid = ((far < row_me) & (row_me + d < rows)) | ((far > row_me) & (row_me - d >= 0))
        pl.when(valid)(lambda k=k: settle(col_all.at[:, 0], z_send.at[k]))
    settle(row_all.at[:, pl.ds(0, chips - 1)], x_send.at[0])
    settle(row_all.at[:, 0], x_send.at[1])
    settle(row_all.at[:, pl.ds(0, chips - 1)], x_send.at[2])


def order_table(row_total):
    table = np.zeros((2 * PSEG * row_total, 2 * PSEG * row_total), np.float32)
    for c in range(2):
        for s in range(PSEG):
            for g in range(row_total):
                at = g // CH_DEV * BLOCK + c * ROWS + g % CH_DEV * PSEG + s
                table[(c * PSEG + s) * row_total + g, at] = 1.0
    return table.astype(jnp.bfloat16)


def pairs_of(outgoing, labels):
    rows, cols = lax.axis_size("row"), lax.axis_size("col")
    row_total, col_total = cols * CH_DEV, rows * CH_DEV
    pairs = row_total * col_total
    flip = np.eye(TILE, dtype=np.float32)[::-1].astype(jnp.bfloat16)
    tables = forward_tables() + lag_tables() + (order_table(row_total), flip)
    consts = [jnp.asarray(t) for t in tables]
    block = (QUADS, BLOCK, F2)
    return pl.pallas_call(
        pair_kernel,
        out_shape=jax.ShapeDtypeStruct((row_total, col_total, LAGS), jnp.bfloat16),
        in_specs=[pl.BlockSpec(memory_space=pltpu.VMEM)] * 2 + [pl.BlockSpec(memory_space=pltpu.HBM)] * len(consts),
        out_specs=pl.BlockSpec(memory_space=pltpu.VMEM),
        scratch_shapes=[pltpu.VMEM(t.shape, t.dtype) for t in consts]
        + [
            pltpu.VMEM(outgoing.shape, jnp.bfloat16),
            pltpu.VMEM(labels.shape, jnp.bfloat16),
            pltpu.VMEM((ROWS, NT), jnp.float32),
            pltpu.VMEM((N1 * ROWS, 2 * N2), jnp.float32),
            pltpu.VMEM((TURNS, TILES, PAIR, TILE), jnp.bfloat16),
            pltpu.VMEM((STEPS, cols) + block, jnp.bfloat16),
            pltpu.VMEM((STEPS, rows) + block, jnp.bfloat16),
            pltpu.VMEM((QUADS, 2 * PSEG, row_total, F2), jnp.bfloat16),
            pltpu.VMEM((QUADS, rows * BLOCK, F2), jnp.float32),
            pltpu.VMEM((2, 2, QUADS, pairs, F2), jnp.bfloat16),
            pltpu.VMEM((TILES, 2, pairs, F2), jnp.float32),
            pltpu.VMEM((TILES // 2, 2, pairs, F2), jnp.bfloat16),
            pltpu.SemaphoreType.DMA((PARTS + 1,)),
            pltpu.SemaphoreType.DMA((PARTS,)),
            pltpu.SemaphoreType.DMA,
            pltpu.SemaphoreType.DMA((3 * (rows // 2),)),
            pltpu.SemaphoreType.DMA((STEPS,)),
            pltpu.SemaphoreType.DMA((STEPS,)),
            pltpu.SemaphoreType.DMA((3,)),
            pltpu.SemaphoreType.DMA((STEPS,)),
            pltpu.SemaphoreType.DMA((STEPS,)),
            pltpu.SemaphoreType.DMA((len(consts),)),
        ],
        compiler_params=pltpu.CompilerParams(
            vmem_limit_bytes=44 << 20, collective_id=0, has_side_effects=True
        ),
    )(outgoing, labels, *consts)


def local(strain, file_channels, file_counts, window_start):
    row_count = lax.axis_size("row")
    col_count = lax.axis_size("col")
    my_row = lax.axis_index("row")
    my_col = lax.axis_index("col")
    slot_total = strain.shape[0]
    window = lax.dynamic_slice_in_dim(strain, window_start[0], SEGS * NT, 1)
    slot_index = jnp.arange(slot_total, dtype=jnp.int32)
    live_slot = slot_index < file_counts[0]
    owner_row = file_channels // CH_DEV // col_count
    local_slot = file_channels % CH_DEV
    same_owner = (owner_row[:, None] == owner_row[None, :]) & live_slot[None, :]
    earlier = slot_index[None, :] < slot_index[:, None]
    position = jnp.sum((same_owner & earlier).astype(jnp.int32), axis=1)
    target = owner_row * CAP + position
    routing = (
        jnp.arange(row_count * CAP, dtype=jnp.int32)[:, None] == target[None, :]
    ) & live_slot[None, :]
    outgoing = jnp.dot(
        routing.astype(jnp.bfloat16), window, preferred_element_type=jnp.float32
    ).astype(jnp.bfloat16)
    labels = jnp.sum(jnp.where(routing, local_slot[None, :] + 1, 0), axis=1) - 1
    outgoing = outgoing.reshape(row_count, CAP, PARTS, PSEG, NT).transpose(2, 0, 1, 3, 4)
    labels = jnp.broadcast_to(labels.astype(jnp.bfloat16)[:, None, None], (row_count * CAP, PSEG, 128))
    return pairs_of(
        outgoing.reshape(PARTS, row_count, CAP * PSEG, NT), labels.reshape(row_count, CAP * PSEG, 128)
    )


def solution(mesh):
    placed = (P(("row", "col"), None), P(("row", "col")), P(("row", "col")), P(("row", "col")))
    return jax.shard_map(
        local, mesh=mesh, in_specs=placed, out_specs=P("row", "col", None), check_vma=False
    )
```

```python
import functools
import math

import jax
import jax.numpy as jnp
import numpy as np
from jax import lax
from jax.experimental import pallas as pl
from jax.experimental.pallas import tpu as pltpu
from jax.sharding import PartitionSpec as P

NF = 2048
NT = 4096
LAGS = 1024
SEGS = 8
CH_DEV = 4
CAP = 2
SMOOTH = 32
EDGE = 128
N1 = 16
N2 = NT // N1
F2 = NF // N1
HALF = LAGS // 2
PARTS = 2
PSEG = SEGS // PARTS
ROWS = CH_DEV * PSEG
BLOCK = 2 * ROWS
QUADS = 4
PAIR = QUADS * F2
TURNS = NF // PAIR
STEPS = PARTS * TURNS
TILE = 256
TILES = 2 * HALF // TILE
CORES = 2
LEAD = 2
MESH = pl.DeviceIdType.MESH


def wave(k, period):
    bits = period.bit_length() - 1
    k = k & (period - 1)
    quarter = (4 * k + period // 2) >> bits
    r = (4 * k - (quarter << bits)).astype(jnp.float32) * np.float32(0.5 * np.pi / period)
    r2 = r * r
    odd = r * (1 + r2 * (-1 / 6 + r2 * (1 / 120 + r2 * (-1 / 5040 + r2 * (1 / 362880)))))
    even = 1 + r2 * (-1 / 2 + r2 * (1 / 24 + r2 * (-1 / 720 + r2 * (1 / 40320))))
    swap = (quarter & 1) == 1
    c, s = jnp.where(swap, odd, even), jnp.where(swap, even, odd)
    return jnp.where(((quarter + 1) & 2) == 2, -c, c), jnp.where((quarter & 2) == 2, -s, s)


def grid(shape):
    return [lax.broadcasted_iota(jnp.int32, shape, n) for n in range(2)]


def forward_tables(tw_ref, hi_ref, lo_ref, shape_ref):
    f1, n2 = grid((N1, N2))
    c, s = wave(f1 * n2, NT)
    tw_ref[0], tw_ref[1] = c, -s
    n2, f2 = grid((N2, F2))
    c, s = wave(n2 * f2, N2)
    for block, (r, l) in ((c, (0, 0)), (-s, (0, 1)), (s, (1, 0)), (c, (1, 1))):
        high = block.astype(jnp.bfloat16)
        at = slice(r * N2, (r + 1) * N2), slice(l * F2, (l + 1) * F2)
        hi_ref[at] = high
        lo_ref[at] = (block - high.astype(jnp.float32)).astype(jnp.bfloat16)
    f1, f2 = grid((N1, F2))
    f = f1 + N1 * f2
    c, s = wave(f, 2 * NT)
    rise = wave(jnp.minimum(jnp.minimum(2 * f + 1, 2 * NF - 2 * f - 1), 2 * EDGE), 8 * EDGE)[1]
    shape_ref[0], shape_ref[1], shape_ref[2] = rise * rise, c, -s


def lag_tables(w_ref):
    for k in range(HALF // TILE):
        f2, m = grid((F2, TILE))
        bc, bs = wave(N1 * f2 * (2 * (m + k * TILE) + 1), 2 * NT)
        f1, m = grid((N1, TILE))
        fc, fs = wave(f1 * (2 * (m + k * TILE) + 1), 2 * NT)
        for f in range(N1):
            ac, as_ = fc[f : f + 1], fs[f : f + 1]
            t, at = f * F2 // PAIR, slice(f * F2 % PAIR, f * F2 % PAIR + F2)
            w_ref[t, k, at, :] = (ac * bc - as_ * bs).astype(jnp.bfloat16)
            w_ref[t, HALF // TILE + k, at, :] = (-(as_ * bc + ac * bs)).astype(jnp.bfloat16)


def order_tables(perm_ref, flip_ref, row_total):
    row, lane = grid((perm_ref.shape[0], F2))
    k, g = lax.div(row, row_total), lax.rem(row, row_total)
    c, s = lax.div(k, PSEG), lax.rem(k, PSEG)
    at = lax.div(g, CH_DEV) * BLOCK + c * ROWS + lax.rem(g, CH_DEV) * PSEG + s
    for n in range(perm_ref.shape[1] // F2):
        perm_ref[:, n * F2 : (n + 1) * F2] = jnp.where(at == lane + n * F2, 1.0, 0.0).astype(jnp.bfloat16)
    row, lane = grid((TILE, TILE))
    flip_ref[...] = jnp.where(row + lane == TILE - 1, 1.0, 0.0).astype(jnp.bfloat16)


def shifted(value, lanes, amount):
    rolled = pltpu.roll(value, amount % F2, 1)
    source = lanes - amount
    return jnp.where((source >= 0) & (source < F2), rolled, 0.0)


def greet(axes):
    barrier = pltpu.get_barrier_semaphore()
    count = 0
    for axis in axes:
        size, me = lax.axis_size(axis), lax.axis_index(axis)
        for d in range(1, size):
            pl.semaphore_signal(barrier, inc=1, device_id={axis: lax.rem(me + d, size)}, device_id_type=MESH)
            count += 1
    pl.semaphore_wait(barrier, count)


def tree(terms):
    while len(terms) > 1:
        terms = [terms[k] + terms[k + 1] for k in range(0, len(terms), 2)]
    return terms[0]


def combine(values, weights):
    total = None
    for v, w in zip(values, weights):
        if abs(w) < 1e-9:
            continue
        term = v if abs(w - 1) < 1e-9 else (-v if abs(w + 1) < 1e-9 else v * np.float32(w))
        total = term if total is None else total + term
    return total


def dot(a, b):
    return jnp.dot(a, b, preferred_element_type=jnp.float32)


def chosen_rows(label):
    count = label.shape[0]
    row = lax.broadcasted_iota(jnp.int32, label.shape, 0)
    lane = lax.broadcasted_iota(jnp.int32, label.shape, 1)
    hit = (label == (lane // PSEG).astype(jnp.float32)) & (lax.rem(row, PSEG) == lax.rem(lane, PSEG))
    picks = jnp.where(hit, 1.0, 0.0)
    if count < 128:
        picks = jnp.concatenate([picks, jnp.zeros((128 - count, 128), jnp.float32)], axis=0)
    return jnp.transpose(picks)[:ROWS, :count].astype(jnp.bfloat16)


def spectra_part(part, picks, got, x_ref, z_ref, tw_ref, hi_ref, lo_ref, shape_ref, put):
    x_ref[...] = dot(picks, got[part].reshape(-1, NT))
    cosines = np.cos(2 * np.pi * np.arange(N1) / N1)
    sines = np.sin(2 * np.pi * np.arange(N1) / N1)
    for h in range(0, N2, 128):
        xs = [x_ref[:, k * N2 + h : k * N2 + h + 128] for k in range(N1)]
        even = [xs[k] + xs[k + N1 // 2] for k in range(N1 // 2)]
        odd = [xs[k] - xs[k + N1 // 2] for k in range(N1 // 2)]
        for f in range(N1 // 2 + 1):
            src = even if f % 2 == 0 else odd
            re = combine(src, [cosines[f * k % N1] for k in range(N1 // 2)])
            im = combine(src, [-sines[f * k % N1] for k in range(N1 // 2)])
            for f1, sign in {f: 1.0, (N1 - f) % N1: -1.0}.items() if f not in (0, N1 // 2) else ((f, 1.0),):
                tc = tw_ref[0, f1 : f1 + 1, h : h + 128]
                ts = tw_ref[1, f1 : f1 + 1, h : h + 128]
                if im is None:
                    zr, zi = re * tc, re * ts
                else:
                    i = im if sign > 0 else -im
                    zr, zi = re * tc - i * ts, re * ts + i * tc
                z_ref[f1 * ROWS : (f1 + 1) * ROWS, h : h + 128] = zr
                z_ref[f1 * ROWS : (f1 + 1) * ROWS, N2 + h : N2 + h + 128] = zi
    z = z_ref[...]
    zh = z.astype(jnp.bfloat16)
    zl = (z - zh.astype(jnp.float32)).astype(jnp.bfloat16)
    z_ref[:, : 2 * F2] = dot(zh, hi_ref[...]) + dot(zl, hi_ref[...]) + dot(zh, lo_ref[...])
    lanes = lax.broadcasted_iota(jnp.int32, (ROWS, F2), 1)
    piece = lambda f1, c: z_ref[f1 * ROWS : (f1 + 1) * ROWS, c * F2 : (c + 1) * F2]
    power = []
    for f1 in range(N1):
        re, im = piece(f1, 0), piece(f1, 1)
        power.append(re * re + im * im)
    prefix, suffix = [power[0]], [power[-1]]
    for k in range(1, N1):
        prefix.append(prefix[-1] + power[k])
        suffix.append(suffix[-1] + power[N1 - 1 - k])
    suffix = suffix[::-1]
    total = prefix[-1]
    reach = SMOOTH // N1
    middle = total
    for k in range(1, reach):
        middle = middle + shifted(total, lanes, k) + shifted(total, lanes, -k)
    for f1 in range(N1):
        window = middle + shifted(suffix[f1], lanes, reach) + shifted(prefix[f1], lanes, -reach)
        scale = shape_ref[0, f1 : f1 + 1] * lax.rsqrt(window * (1.0 / (2 * SMOOTH + 1)) + 1e-06)
        re, im = piece(f1, 0) * scale, piece(f1, 1) * scale
        tc, ts = shape_ref[1, f1 : f1 + 1], shape_ref[2, f1 : f1 + 1]
        put(part * TURNS + f1 // QUADS, f1 % QUADS, re, im, re * tc - im * ts, re * ts + im * tc)


def route(chan_ref, count_ref, cols, height):
    slots = chan_ref.shape[0]
    row = lax.broadcasted_iota(jnp.int32, (height, 128), 0)
    lane = lax.broadcasted_iota(jnp.int32, (height, 128), 1)
    place = lax.div(row, PSEG)
    owners = [lax.div(chan_ref[s], CH_DEV * cols) for s in range(slots)]
    live = [s < count_ref[0] for s in range(slots)]
    picks = jnp.zeros((height, 128), jnp.float32)
    label = jnp.full((height, 128), -1.0, jnp.float32)
    for s in range(slots):
        position = jnp.int32(0)
        for e in range(s):
            position = position + jnp.where(live[e] & (owners[e] == owners[s]), 1, 0)
        target = jnp.where(live[s], owners[s] * CAP + position, -1)
        hit = place == target
        picks = jnp.where(hit & (lax.rem(lane, slots) == s), 1.0, picks)
        label = jnp.where(hit, lax.rem(chan_ref[s], CH_DEV).astype(jnp.float32), label)
    picks = jnp.where(lax.rem(row, PSEG) == lax.div(lane, slots), picks, 0.0)
    return picks[:, : PSEG * slots].astype(jnp.bfloat16), label.astype(jnp.bfloat16)


def pair_kernel(win_ref, chan_ref, count_ref, *refs):
    result, tables, refs = refs[0], refs[1:5], refs[5:]
    perm_ref, flip_ref, refs = refs[0], refs[1], refs[2:]
    out_ref, lab_ref, got, glab, x_ref, z_ref, w_ref, row_all, col_all, v_ref, b32, cross, acc, down_ref = refs[:14]
    a_send, a_recv, lab_recv, z_send, z_recv, x_send, x_same, x_mate = refs[14:]
    rows, cols = lax.axis_size("row"), lax.axis_size("col")
    row_total, col_total = cols * CH_DEV, rows * CH_DEV
    wide = CH_DEV * row_total
    row_me, col_me = lax.axis_index("row"), lax.axis_index("col")
    hops, chips = rows // 2, cols // CORES
    far = lax.rem(row_me + hops, rows)
    chip, core = col_me // CORES, lax.rem(col_me, CORES)
    mate = chip * CORES + (1 - core)
    chip_at = lambda d: lax.rem(chip + chips - d, chips) * CORES

    routing, label = route(chan_ref, count_ref, cols, rows * CAP * PSEG)
    lab_ref[...] = label.reshape(lab_ref.shape)
    for part in range(PARTS):
        window = [win_ref[:, (part * PSEG + k) * NT : (part * PSEG + k + 1) * NT] for k in range(PSEG)]
        moved = dot(routing, jnp.concatenate(window, axis=0)).astype(jnp.bfloat16)
        out_ref[part] = moved.reshape(out_ref.shape[1:])
    greet(("row", "col"))

    def remote(src, dst, send, recv, peer):
        return pltpu.make_async_remote_copy(
            src_ref=src, dst_ref=dst, send_sem=send, recv_sem=recv, device_id=peer, device_id_type=MESH
        )

    def settle(ref, sem):
        pltpu.make_async_copy(ref, ref, sem).wait()

    for d in range(1, rows):
        peer = lax.rem(row_me + d, rows)
        remote(lab_ref.at[peer], glab.at[d], a_send.at[PARTS], lab_recv, {"row": peer}).start()
    for part in range(PARTS):
        for d in range(1, rows):
            peer = lax.rem(row_me + d, rows)
            remote(out_ref.at[part, peer], got.at[part, d], a_send.at[part], a_recv.at[part], {"row": peer}).start()
    glab[0] = lab_ref[row_me]
    for part in range(PARTS):
        got[part, 0] = out_ref[part, row_me]

    last = rows - 1
    far_up, far_down = (far < row_me) & (row_me < last), (far > row_me) & (row_me > 0)
    near_up, near_down = row_me == last - 1, row_me == 1
    near = jnp.where(near_up, row_me - (hops - 1), row_me + (hops - 1))

    def z_copy(u, origin, peer, k):
        block = col_all.at[u, origin]
        return remote(block, block, z_send.at[k], z_recv.at[origin, u], {"row": peer})

    def x_copy(u, origin, peer, k):
        sem = x_same if k == 0 else x_mate
        return remote(row_all.at[u, origin], row_all.at[u, origin], x_send.at[k], sem.at[u], {"col": peer})

    def begin(u, part):
        for d in range(hops, 0, -1):
            up, down = row_me + d, row_me - d
            cut = 1 if part == PARTS - 1 and d == hops and hops > 1 else 0
            pl.when(up <= last - cut)(z_copy(u, row_me, up, 2 * d - 2).start)
            pl.when(down >= cut)(z_copy(u, row_me, down, 2 * d - 1).start)
        for d in range(1, chips):
            x_copy(u, col_me, chip_at(d) + core, 0).start()
        x_copy(u, col_me, mate, 1).start()

    def relay(u):
        settled = lambda origin: settle(col_all.at[u, pl.ds(0, 1)], z_recv.at[origin, u])
        if hops > 1:

            @pl.when((u >= TURNS * (PARTS - 1)) & (near_up | near_down))
            def _():
                settled(near)
                pl.when(near_up)(z_copy(u, near, last, 2 * hops + hops - 1).start)
                pl.when(near_down)(z_copy(u, near, 0, 2 * hops + hops - 1).start)

        @pl.when(far_up | far_down)
        def _():
            settled(far)
            for d in range(1, hops):
                k = 2 * hops + d - 1
                pl.when(far_up & (row_me + d <= last))(z_copy(u, far, row_me + d, k).start)
                pl.when(far_down & (row_me - d >= 0))(z_copy(u, far, row_me - d, k).start)

    def forward(u):
        settle(row_all.at[u, pl.ds(0, chips - 1)], x_same.at[u])
        for d in range(1, chips):
            x_copy(u, chip_at(d) + core, mate, 2).start()

    def origin_of(k):
        origin, bit = row_me, 1
        while bit < rows:
            flip = lax.rem(k // bit, 2)
            origin = origin + flip * bit * (1 - 2 * lax.rem(row_me // bit, 2))
            bit *= 2
        return origin

    def arrive(u):
        settle(row_all.at[u, pl.ds(0, chips)], x_mate.at[u])
        for q in range(0, QUADS, 2):
            sides = [row_all[u, :, q + n].reshape(-1, F2) for n in range(2)]
            turned = dot(perm_ref[...], jnp.concatenate(sides, axis=1)).astype(jnp.bfloat16)
            for n in range(2):
                for j in range(2 * PSEG):
                    v_ref[q + n, j] = turned[j * row_total : (j + 1) * row_total, n * F2 : (n + 1) * F2]

    origins = [origin_of(k) for k in range(rows)]
    relays_far, relays_near = far_up | far_down, near_up | near_down

    def meet(u, part, k, more):
        origin = origins[k]
        if k > 0:
            known = (origin == far) & relays_far
            if hops > 1 and part == PARTS - 1:
                known = known | ((origin == near) & relays_near)

            @pl.when(jnp.logical_not(known))
            def _():
                settle(col_all.at[u, pl.ds(0, 1)], z_recv.at[origin, u])

        if k == 1:
            pl.when(more)(lambda: relay(u + LEAD))
        if k == 2 % rows:
            pl.when(u + LEAD < STEPS)(lambda: forward(u + LEAD))

    def put(u, q, re, im, tr, ti):
        for c, (a, b) in enumerate(((re, tr), (im, ti))):
            at = slice(c * ROWS, (c + 1) * ROWS)
            col_all[u, row_me, q, at] = a.astype(jnp.bfloat16)
            row_all[u, col_me, q, at] = b.astype(jnp.bfloat16)

    def cross_item(u, k):
        origin, now = origins[k], lax.rem(u, TURNS)
        for q in range(QUADS):
            b32[q] = col_all[u, origin, q].astype(jnp.float32)
        for q in range(QUADS):
            for ch in range(CH_DEV):
                spread = lambda r: jnp.broadcast_to(b32[q, r : r + 1, :], (16, F2)).astype(jnp.bfloat16)
                br = [spread(ch * PSEG + s) for s in range(PSEG)]
                bi = [spread(ROWS + ch * PSEG + s) for s in range(PSEG)]
                for g in range(0, row_total, 16):
                    real, imag = [], []
                    for s in range(PSEG):
                        ar, ai = v_ref[q, s, g : g + 16], v_ref[q, PSEG + s, g : g + 16]
                        real.append(br[s] * ar + bi[s] * ai)
                        imag.append(br[s] * ai - bi[s] * ar)
                    line = pl.ds(pl.multiple_of(origin * wide + ch * row_total + g, 16), 16)
                    cross[now, 0, q, line] = tree(real)
                    cross[now, 1, q, line] = tree(imag)

    def lags(first, count, fresh, beside=None):
        @pl.loop(0, TILES)
        def _(i):
            if beside is not None:
                beside(i)
            side = [cross[first + n, i // (TILES // 2), q] for n in range(count) for q in range(QUADS)]
            table = w_ref[pl.ds(first, count), i].reshape(count * PAIR, TILE)
            term = dot(jnp.concatenate(side, axis=1), table)
            for h in range(2):
                piece = term[:, h * F2 : (h + 1) * F2]
                acc[i, h] = piece if fresh else acc[i, h] + piece

    forward_tables(*tables)
    lag_tables(w_ref)
    order_tables(perm_ref, flip_ref, row_total)
    settle(glab.at[pl.ds(1, rows - 1)], lab_recv)
    settle(got.at[0, pl.ds(1, rows - 1)], a_recv.at[0])
    picks = chosen_rows(glab[...].reshape(-1, 128).astype(jnp.float32))
    spectra_part(0, picks, got, x_ref, z_ref, *tables, put)

    @pl.loop(0, TURNS)
    def _(u):
        begin(u, 0)

    for u in range(LEAD):
        forward(u)
    settle(got.at[1, pl.ds(1, rows - 1)], a_recv.at[1])
    spectra_part(1, picks, got, x_ref, z_ref, *tables, put)

    @pl.loop(TURNS, STEPS)
    def _(u):
        begin(u, 1)

    for u in range(LEAD):
        relay(u)

    def step(u, part, more):
        arrive(u)
        for k in range(rows):
            meet(u, part, k, more)
            cross_item(u, k)

    @pl.loop(0, TURNS)
    def _(u):
        step(u, 0, u + LEAD < TURNS)

    def beside(i):
        @pl.when(lax.rem(i, TILES // LEAD) == 0)
        def _():
            relay(TURNS + i // (TILES // LEAD))

    lags(0, TURNS, True, beside)

    @pl.loop(0, TURNS // 2)
    def _(p):
        @pl.loop(0, 2)
        def _(n):
            u = TURNS + 2 * p + n
            step(u, 1, u + LEAD < STEPS)

        lags(2 * p, 2, False)

    half = TILES // 2
    place = lax.broadcasted_iota(jnp.int32, (col_total, F2), 0)
    scale = np.float32(1.0 / math.sqrt(SEGS * NF))

    @pl.loop(0, row_total)
    def _(g):
        own = g - col_me * CH_DEV
        mine = (place == row_me * CH_DEV + own) & (own >= 0) & (own < CH_DEV)
        keep = jnp.where(mine, 0.0, scale)
        for k in range(half):
            for n in range(2):
                a = acc[k, n, pl.ds(g, col_total, stride=row_total), :]
                b = acc[half + k, n, pl.ds(g, col_total, stride=row_total), :]
                first = HALF + k * TILE + n * F2
                result[g, :, first : first + F2] = ((a + b) * keep).astype(jnp.bfloat16)
                down_ref[k, n, pl.ds(pl.multiple_of(g * col_total, 16), col_total), :] = ((a - b) * keep).astype(jnp.bfloat16)

    for k in range(half):
        side = jnp.concatenate([down_ref[k, n] for n in range(2)], axis=1)
        turned = dot(side, flip_ref[...]).astype(jnp.bfloat16)
        result[:, :, HALF - (k + 1) * TILE : HALF - k * TILE] = turned.reshape(row_total, col_total, TILE)

    settle(glab.at[pl.ds(1, rows - 1)], a_send.at[PARTS])
    for part in range(PARTS):
        settle(got.at[part, pl.ds(1, rows - 1)], a_send.at[part])
    whole, short = col_all.at[:, 0], col_all.at[pl.ds(0, STEPS - TURNS), 0]
    for d in range(1, hops + 1):
        cut = 1 if d == hops and hops > 1 else 0
        up, down = row_me + d, row_me - d
        pl.when(up <= last - cut)(lambda k=2 * d - 2: settle(whole, z_send.at[k]))
        pl.when(down >= cut)(lambda k=2 * d - 1: settle(whole, z_send.at[k]))
        if cut:
            pl.when(up == last)(lambda k=2 * d - 2: settle(short, z_send.at[k]))
            pl.when(down == 0)(lambda k=2 * d - 1: settle(short, z_send.at[k]))
    for d in range(1, hops):
        sent = (far_up & (row_me + d <= last)) | (far_down & (row_me - d >= 0))
        pl.when(sent)(lambda k=2 * hops + d - 1: settle(whole, z_send.at[k]))
    if hops > 1:
        pl.when(near_up | near_down)(lambda: settle(short, z_send.at[3 * hops - 1]))
    settle(row_all.at[:, pl.ds(0, chips - 1)], x_send.at[0])
    settle(row_all.at[:, 0], x_send.at[1])
    settle(row_all.at[:, pl.ds(0, chips - 1)], x_send.at[2])


def pairs_of(window, file_channels, file_counts):
    rows, cols = lax.axis_size("row"), lax.axis_size("col")
    row_total, col_total = cols * CH_DEV, rows * CH_DEV
    pairs = row_total * col_total
    order = 2 * PSEG * row_total
    block = (QUADS, BLOCK, F2)
    return pl.pallas_call(
        pair_kernel,
        out_shape=jax.ShapeDtypeStruct((row_total, col_total, LAGS), jnp.bfloat16),
        in_specs=[pl.BlockSpec(memory_space=pltpu.VMEM)] + [pl.BlockSpec(memory_space=pltpu.SMEM)] * 2,
        out_specs=pl.BlockSpec(memory_space=pltpu.VMEM),
        scratch_shapes=[
            pltpu.VMEM((2, N1, N2), jnp.float32),
            pltpu.VMEM((2 * N2, 2 * F2), jnp.bfloat16),
            pltpu.VMEM((2 * N2, 2 * F2), jnp.bfloat16),
            pltpu.VMEM((3, N1, F2), jnp.float32),
            pltpu.VMEM((order, order), jnp.bfloat16),
            pltpu.VMEM((TILE, TILE), jnp.bfloat16),
            pltpu.VMEM((PARTS, rows, CAP * PSEG, NT), jnp.bfloat16),
            pltpu.VMEM((rows, CAP * PSEG, 128), jnp.bfloat16),
            pltpu.VMEM((PARTS, rows, CAP * PSEG, NT), jnp.bfloat16),
            pltpu.VMEM((rows, CAP * PSEG, 128), jnp.bfloat16),
            pltpu.VMEM((ROWS, NT), jnp.float32),
            pltpu.VMEM((N1 * ROWS, 2 * N2), jnp.float32),
            pltpu.VMEM((TURNS, TILES, PAIR, TILE), jnp.bfloat16),
            pltpu.VMEM((STEPS, cols) + block, jnp.bfloat16),
            pltpu.VMEM((STEPS, rows) + block, jnp.bfloat16),
            pltpu.VMEM((QUADS, 2 * PSEG, row_total, F2), jnp.bfloat16),
            pltpu.VMEM((QUADS, BLOCK, F2), jnp.float32),
            pltpu.VMEM((TURNS, 2, QUADS, pairs, F2), jnp.bfloat16),
            pltpu.VMEM((TILES, 2, pairs, F2), jnp.float32),
            pltpu.VMEM((TILES // 2, 2, pairs, F2), jnp.bfloat16),
            pltpu.SemaphoreType.DMA((PARTS + 1,)),
            pltpu.SemaphoreType.DMA((PARTS,)),
            pltpu.SemaphoreType.DMA,
            pltpu.SemaphoreType.DMA((3 * (rows // 2),)),
            pltpu.SemaphoreType.DMA((rows, STEPS)),
            pltpu.SemaphoreType.DMA((3,)),
            pltpu.SemaphoreType.DMA((STEPS,)),
            pltpu.SemaphoreType.DMA((STEPS,)),
        ],
        compiler_params=pltpu.CompilerParams(
            vmem_limit_bytes=48 << 20, collective_id=0, has_side_effects=True
        ),
    )(window, file_channels, file_counts)


def local(strain, file_channels, file_counts, window_start):
    window = lax.dynamic_slice_in_dim(strain, window_start[0], SEGS * NT, 1)
    return pairs_of(window, file_channels, file_counts)


def solution(mesh):
    placed = (P(("row", "col"), None), P(("row", "col")), P(("row", "col")), P(("row", "col")))
    return jax.shard_map(
        local, mesh=mesh, in_specs=placed, out_specs=P("row", "col", None), check_vma=False
    )
```

```python
import functools
import math

import jax
import jax.numpy as jnp
import numpy as np
from jax import lax
from jax.experimental import pallas as pl
from jax.experimental.pallas import tpu as pltpu
from jax.sharding import PartitionSpec as P

NF = 2048
NT = 4096
LAGS = 1024
SEGS = 8
CH_DEV = 4
CAP = 2
SMOOTH = 32
EDGE = 128
N1 = 16
N2 = NT // N1
F2 = NF // N1
HALF = LAGS // 2
PARTS = 2
PSEG = SEGS // PARTS
ROWS = CH_DEV * PSEG
BLOCK = 2 * ROWS
QUADS = 4
PAIR = QUADS * F2
TURNS = NF // PAIR
STEPS = PARTS * TURNS
TILE = 256
TILES = 2 * HALF // TILE
CORES = 2
LEAD = 2
MESH = pl.DeviceIdType.MESH


def wave(k, period):
    bits = period.bit_length() - 1
    k = k & (period - 1)
    quarter = (4 * k + period // 2) >> bits
    r = (4 * k - (quarter << bits)).astype(jnp.float32) * np.float32(0.5 * np.pi / period)
    r2 = r * r
    odd = r * (1 + r2 * (-1 / 6 + r2 * (1 / 120 + r2 * (-1 / 5040 + r2 * (1 / 362880)))))
    even = 1 + r2 * (-1 / 2 + r2 * (1 / 24 + r2 * (-1 / 720 + r2 * (1 / 40320))))
    swap = (quarter & 1) == 1
    c, s = jnp.where(swap, odd, even), jnp.where(swap, even, odd)
    return jnp.where(((quarter + 1) & 2) == 2, -c, c), jnp.where((quarter & 2) == 2, -s, s)


def grid(shape):
    return [lax.broadcasted_iota(jnp.int32, shape, n) for n in range(2)]


def forward_tables(tw_ref, hi_ref, lo_ref, shape_ref):
    f1, n2 = grid((N1, N2))
    c, s = wave(f1 * n2, NT)
    tw_ref[0], tw_ref[1] = c, -s
    n2, f2 = grid((N2, F2))
    c, s = wave(n2 * f2, N2)
    for block, (r, l) in ((c, (0, 0)), (-s, (0, 1)), (s, (1, 0)), (c, (1, 1))):
        high = block.astype(jnp.bfloat16)
        at = slice(r * N2, (r + 1) * N2), slice(l * F2, (l + 1) * F2)
        hi_ref[at] = high
        lo_ref[at] = (block - high.astype(jnp.float32)).astype(jnp.bfloat16)
    f1, f2 = grid((N1, F2))
    f = f1 + N1 * f2
    c, s = wave(f, 2 * NT)
    rise = wave(jnp.minimum(jnp.minimum(2 * f + 1, 2 * NF - 2 * f - 1), 2 * EDGE), 8 * EDGE)[1]
    shape_ref[0], shape_ref[1], shape_ref[2] = rise * rise, c, -s


def lag_tables(w_ref):
    scale = np.float32(1.0 / math.sqrt(SEGS * NF))
    for k in range(HALF // TILE):
        f2, m = grid((F2, TILE))
        bc, bs = wave(N1 * f2 * (2 * (m + k * TILE) + 1), 2 * NT)
        f1, m = grid((N1, TILE))
        fc, fs = [v * scale for v in wave(f1 * (2 * (m + k * TILE) + 1), 2 * NT)]
        for f in range(N1):
            ac, as_ = fc[f : f + 1], fs[f : f + 1]
            t, at = f * F2 // PAIR, slice(f * F2 % PAIR, f * F2 % PAIR + F2)
            w_ref[t, k, at, :] = (ac * bc - as_ * bs).astype(jnp.bfloat16)
            w_ref[t, HALF // TILE + k, at, :] = (-(as_ * bc + ac * bs)).astype(jnp.bfloat16)


def order_tables(perm_ref, flip_ref, row_total):
    row, lane = grid((perm_ref.shape[0], F2))
    k, g = lax.div(row, row_total), lax.rem(row, row_total)
    c, s = lax.div(k, PSEG), lax.rem(k, PSEG)
    at = lax.div(g, CH_DEV) * BLOCK + c * ROWS + lax.rem(g, CH_DEV) * PSEG + s
    for n in range(perm_ref.shape[1] // F2):
        perm_ref[:, n * F2 : (n + 1) * F2] = jnp.where(at == lane + n * F2, 1.0, 0.0).astype(jnp.bfloat16)
    row, lane = grid((TILE, TILE))
    flip_ref[...] = jnp.where(row + lane == TILE - 1, 1.0, 0.0).astype(jnp.bfloat16)


def shifted(value, lanes, amount):
    rolled = pltpu.roll(value, amount % F2, 1)
    source = lanes - amount
    return jnp.where((source >= 0) & (source < F2), rolled, 0.0)


def greet(axes):
    barrier = pltpu.get_barrier_semaphore()
    count = 0
    for axis in axes:
        size, me = lax.axis_size(axis), lax.axis_index(axis)
        for d in range(1, size):
            pl.semaphore_signal(barrier, inc=1, device_id={axis: lax.rem(me + d, size)}, device_id_type=MESH)
            count += 1
    pl.semaphore_wait(barrier, count)


def tree(terms):
    while len(terms) > 1:
        terms = [terms[k] + terms[k + 1] for k in range(0, len(terms), 2)]
    return terms[0]


def combine(values, weights):
    total = None
    for v, w in zip(values, weights):
        if abs(w) < 1e-9:
            continue
        term = v if abs(w - 1) < 1e-9 else (-v if abs(w + 1) < 1e-9 else v * np.float32(w))
        total = term if total is None else total + term
    return total


def dot(a, b):
    return jnp.dot(a, b, preferred_element_type=jnp.float32)


def chosen_rows(label):
    count = label.shape[0]
    row = lax.broadcasted_iota(jnp.int32, label.shape, 0)
    lane = lax.broadcasted_iota(jnp.int32, label.shape, 1)
    hit = (label == (lane // PSEG).astype(jnp.float32)) & (lax.rem(row, PSEG) == lax.rem(lane, PSEG))
    picks = jnp.where(hit, 1.0, 0.0)
    if count < 128:
        picks = jnp.concatenate([picks, jnp.zeros((128 - count, 128), jnp.float32)], axis=0)
    return jnp.transpose(picks)[:ROWS, :count].astype(jnp.bfloat16)


def spectra_part(part, picks, got, x_ref, z_ref, tw_ref, hi_ref, lo_ref, shape_ref, put):
    x_ref[...] = dot(picks, got[part].reshape(-1, NT))
    cosines = np.cos(2 * np.pi * np.arange(N1) / N1)
    sines = np.sin(2 * np.pi * np.arange(N1) / N1)
    for h in range(0, N2, 128):
        xs = [x_ref[:, k * N2 + h : k * N2 + h + 128] for k in range(N1)]
        even = [xs[k] + xs[k + N1 // 2] for k in range(N1 // 2)]
        odd = [xs[k] - xs[k + N1 // 2] for k in range(N1 // 2)]
        for f in range(N1 // 2 + 1):
            src = even if f % 2 == 0 else odd
            re = combine(src, [cosines[f * k % N1] for k in range(N1 // 2)])
            im = combine(src, [-sines[f * k % N1] for k in range(N1 // 2)])
            for f1, sign in {f: 1.0, (N1 - f) % N1: -1.0}.items() if f not in (0, N1 // 2) else ((f, 1.0),):
                tc = tw_ref[0, f1 : f1 + 1, h : h + 128]
                ts = tw_ref[1, f1 : f1 + 1, h : h + 128]
                if im is None:
                    zr, zi = re * tc, re * ts
                else:
                    i = im if sign > 0 else -im
                    zr, zi = re * tc - i * ts, re * ts + i * tc
                z_ref[f1 * ROWS : (f1 + 1) * ROWS, h : h + 128] = zr
                z_ref[f1 * ROWS : (f1 + 1) * ROWS, N2 + h : N2 + h + 128] = zi
    z = z_ref[...]
    zh = z.astype(jnp.bfloat16)
    zl = (z - zh.astype(jnp.float32)).astype(jnp.bfloat16)
    z_ref[:, : 2 * F2] = dot(zh, hi_ref[...]) + dot(zl, hi_ref[...]) + dot(zh, lo_ref[...])
    lanes = lax.broadcasted_iota(jnp.int32, (ROWS, F2), 1)
    piece = lambda f1, c: z_ref[f1 * ROWS : (f1 + 1) * ROWS, c * F2 : (c + 1) * F2]
    power = []
    for f1 in range(N1):
        re, im = piece(f1, 0), piece(f1, 1)
        power.append(re * re + im * im)
    prefix, suffix = [power[0]], [power[-1]]
    for k in range(1, N1):
        prefix.append(prefix[-1] + power[k])
        suffix.append(suffix[-1] + power[N1 - 1 - k])
    suffix = suffix[::-1]
    total = prefix[-1]
    reach = SMOOTH // N1
    middle = total
    for k in range(1, reach):
        middle = middle + shifted(total, lanes, k) + shifted(total, lanes, -k)
    for f1 in range(N1):
        window = middle + shifted(suffix[f1], lanes, reach) + shifted(prefix[f1], lanes, -reach)
        scale = shape_ref[0, f1 : f1 + 1] * lax.rsqrt(window * (1.0 / (2 * SMOOTH + 1)) + 1e-06)
        re, im = piece(f1, 0) * scale, piece(f1, 1) * scale
        tc, ts = shape_ref[1, f1 : f1 + 1], shape_ref[2, f1 : f1 + 1]
        put(part * TURNS + f1 // QUADS, f1 % QUADS, re, im, re * tc - im * ts, re * ts + im * tc)


def route(chan_ref, count_ref, cols, height):
    slots = chan_ref.shape[0]
    row = lax.broadcasted_iota(jnp.int32, (height, 128), 0)
    lane = lax.broadcasted_iota(jnp.int32, (height, 128), 1)
    place = lax.div(row, PSEG)
    owners = [lax.div(chan_ref[s], CH_DEV * cols) for s in range(slots)]
    live = [s < count_ref[0] for s in range(slots)]
    picks = jnp.zeros((height, 128), jnp.float32)
    label = jnp.full((height, 128), -1.0, jnp.float32)
    for s in range(slots):
        position = jnp.int32(0)
        for e in range(s):
            position = position + jnp.where(live[e] & (owners[e] == owners[s]), 1, 0)
        target = jnp.where(live[s], owners[s] * CAP + position, -1)
        hit = place == target
        picks = jnp.where(hit & (lax.rem(lane, slots) == s), 1.0, picks)
        label = jnp.where(hit, lax.rem(chan_ref[s], CH_DEV).astype(jnp.float32), label)
    picks = jnp.where(lax.rem(row, PSEG) == lax.div(lane, slots), picks, 0.0)
    return picks[:, : PSEG * slots].astype(jnp.bfloat16), label.astype(jnp.bfloat16)


def pair_kernel(win_ref, chan_ref, count_ref, *refs):
    result, tables, refs = refs[0], refs[1:5], refs[5:]
    perm_ref, flip_ref, refs = refs[0], refs[1], refs[2:]
    out_ref, lab_ref, got, glab, x_ref, z_ref, w_ref, row_all, col_all, v_ref, b32, cross, acc, down_ref = refs[:14]
    a_send, a_recv, lab_recv, z_send, z_recv, x_send, x_same, x_mate = refs[14:]
    rows, cols = lax.axis_size("row"), lax.axis_size("col")
    row_total, col_total = cols * CH_DEV, rows * CH_DEV
    wide = CH_DEV * row_total
    row_me, col_me = lax.axis_index("row"), lax.axis_index("col")
    hops, chips = rows // 2, cols // CORES
    far = lax.rem(row_me + hops, rows)
    chip, core = col_me // CORES, lax.rem(col_me, CORES)
    mate = chip * CORES + (1 - core)
    chip_at = lambda d: lax.rem(chip + chips - d, chips) * CORES

    routing, label = route(chan_ref, count_ref, cols, rows * CAP * PSEG)
    lab_ref[...] = label.reshape(lab_ref.shape)
    for part in range(PARTS):
        window = [win_ref[:, (part * PSEG + k) * NT : (part * PSEG + k + 1) * NT] for k in range(PSEG)]
        moved = dot(routing, jnp.concatenate(window, axis=0)).astype(jnp.bfloat16)
        out_ref[part] = moved.reshape(out_ref.shape[1:])
    greet(("row", "col"))

    def remote(src, dst, send, recv, peer):
        return pltpu.make_async_remote_copy(
            src_ref=src, dst_ref=dst, send_sem=send, recv_sem=recv, device_id=peer, device_id_type=MESH
        )

    def settle(ref, sem):
        pltpu.make_async_copy(ref, ref, sem).wait()

    for d in range(1, rows):
        peer = lax.rem(row_me + d, rows)
        remote(lab_ref.at[peer], glab.at[d], a_send.at[PARTS], lab_recv, {"row": peer}).start()
    for part in range(PARTS):
        for d in range(1, rows):
            peer = lax.rem(row_me + d, rows)
            remote(out_ref.at[part, peer], got.at[part, d], a_send.at[part], a_recv.at[part], {"row": peer}).start()
    glab[0] = lab_ref[row_me]
    for part in range(PARTS):
        got[part, 0] = out_ref[part, row_me]

    last = rows - 1
    far_up, far_down = (far < row_me) & (row_me < last), (far > row_me) & (row_me > 0)
    near_up, near_down = row_me == last - 1, row_me == 1
    near = jnp.where(near_up, row_me - (hops - 1), row_me + (hops - 1))

    def z_copy(u, origin, peer, k):
        block = col_all.at[u, origin]
        return remote(block, block, z_send.at[k], z_recv.at[origin, u], {"row": peer})

    def x_copy(u, origin, peer, k):
        sem = x_same if k == 0 else x_mate
        return remote(row_all.at[u, origin], row_all.at[u, origin], x_send.at[k], sem.at[u], {"col": peer})

    def begin(u, part):
        for d in range(hops, 0, -1):
            up, down = row_me + d, row_me - d
            cut = 1 if part == PARTS - 1 and d == hops and hops > 1 else 0
            pl.when(up <= last - cut)(z_copy(u, row_me, up, 2 * d - 2).start)
            pl.when(down >= cut)(z_copy(u, row_me, down, 2 * d - 1).start)
        for d in range(1, chips):
            x_copy(u, col_me, chip_at(d) + core, 0).start()
        x_copy(u, col_me, mate, 1).start()

    def relay(u):
        settled = lambda origin: settle(col_all.at[u, pl.ds(0, 1)], z_recv.at[origin, u])
        if hops > 1:

            @pl.when((u >= TURNS * (PARTS - 1)) & (near_up | near_down))
            def _():
                settled(near)
                pl.when(near_up)(z_copy(u, near, last, 2 * hops + hops - 1).start)
                pl.when(near_down)(z_copy(u, near, 0, 2 * hops + hops - 1).start)

        @pl.when(far_up | far_down)
        def _():
            settled(far)
            for d in range(1, hops):
                k = 2 * hops + d - 1
                pl.when(far_up & (row_me + d <= last))(z_copy(u, far, row_me + d, k).start)
                pl.when(far_down & (row_me - d >= 0))(z_copy(u, far, row_me - d, k).start)

    def forward(u):
        settle(row_all.at[u, pl.ds(0, chips - 1)], x_same.at[u])
        for d in range(1, chips):
            x_copy(u, chip_at(d) + core, mate, 2).start()

    def origin_of(k):
        origin, bit = row_me, 1
        while bit < rows:
            flip = lax.rem(k // bit, 2)
            origin = origin + flip * bit * (1 - 2 * lax.rem(row_me // bit, 2))
            bit *= 2
        return origin

    def arrive(u):
        settle(row_all.at[u, pl.ds(0, chips)], x_mate.at[u])
        for q in range(0, QUADS, 2):
            sides = [row_all[u, :, q + n].reshape(-1, F2) for n in range(2)]
            turned = dot(perm_ref[...], jnp.concatenate(sides, axis=1)).astype(jnp.bfloat16)
            for n in range(2):
                for j in range(2 * PSEG):
                    v_ref[q + n, j] = turned[j * row_total : (j + 1) * row_total, n * F2 : (n + 1) * F2]

    origins = [origin_of(k) for k in range(rows)]
    relays_far, relays_near = far_up | far_down, near_up | near_down

    def meet(u, part, k, more):
        origin = origins[k]
        if k > 0:
            known = (origin == far) & relays_far
            if hops > 1 and part == PARTS - 1:
                known = known | ((origin == near) & relays_near)

            @pl.when(jnp.logical_not(known))
            def _():
                settle(col_all.at[u, pl.ds(0, 1)], z_recv.at[origin, u])

        if k == 1:
            if more is not False:
                pl.when(more)(lambda: relay(u + LEAD))
        if k == 2 % rows:
            if more is not False:
                pl.when(u + LEAD < STEPS)(lambda: forward(u + LEAD))

    def put(u, q, re, im, tr, ti):
        for c, (a, b) in enumerate(((re, tr), (im, ti))):
            at = slice(c * ROWS, (c + 1) * ROWS)
            col_all[u, row_me, q, at] = a.astype(jnp.bfloat16)
            row_all[u, col_me, q, at] = b.astype(jnp.bfloat16)

    def cross_item(u, k):
        origin, now = origins[k], lax.rem(u, TURNS)
        for q in range(QUADS):
            b32[q] = col_all[u, origin, q].astype(jnp.float32)
        for q in range(QUADS):
            for ch in range(CH_DEV):
                spread = lambda r: jnp.broadcast_to(b32[q, r : r + 1, :], (16, F2)).astype(jnp.bfloat16)
                br = [spread(ch * PSEG + s) for s in range(PSEG)]
                bi = [spread(ROWS + ch * PSEG + s) for s in range(PSEG)]
                for g in range(0, row_total, 16):
                    real, imag = [], []
                    for s in range(PSEG):
                        ar, ai = v_ref[q, s, g : g + 16], v_ref[q, PSEG + s, g : g + 16]
                        real.append(br[s] * ar + bi[s] * ai)
                        imag.append(br[s] * ai - bi[s] * ar)
                    line = pl.ds(pl.multiple_of(origin * wide + ch * row_total + g, 16), 16)
                    cross[now, 0, q, line] = tree(real)
                    cross[now, 1, q, line] = tree(imag)

    def lags(first, count, fresh, beside=None):
        for i in range(TILES):
            if beside is not None:
                beside(i)
            side = [cross[first + n, i // (TILES // 2), q] for n in range(count) for q in range(QUADS)]
            table = w_ref[pl.ds(first, count), i].reshape(count * PAIR, TILE)
            term = dot(jnp.concatenate(side, axis=1), table)
            for h in range(2):
                piece = term[:, h * F2 : (h + 1) * F2]
                acc[i, h] = piece if fresh else acc[i, h] + piece

    forward_tables(*tables)
    lag_tables(w_ref)
    order_tables(perm_ref, flip_ref, row_total)
    settle(glab.at[pl.ds(1, rows - 1)], lab_recv)
    settle(got.at[0, pl.ds(1, rows - 1)], a_recv.at[0])
    picks = chosen_rows(glab[...].reshape(-1, 128).astype(jnp.float32))
    spectra_part(0, picks, got, x_ref, z_ref, *tables, put)

    @pl.loop(0, TURNS)
    def _(u):
        begin(u, 0)

    for u in range(LEAD):
        forward(u)
    settle(got.at[1, pl.ds(1, rows - 1)], a_recv.at[1])
    spectra_part(1, picks, got, x_ref, z_ref, *tables, put)

    @pl.loop(TURNS, STEPS)
    def _(u):
        begin(u, 1)

    for u in range(LEAD):
        relay(u)

    def step(u, part, more):
        arrive(u)
        for k in range(rows):
            meet(u, part, k, more)
            cross_item(u, k)

    @pl.loop(0, TURNS)
    def _(u):
        step(u, 0, u + LEAD < TURNS)

    def beside(i):
        if i % (TILES // LEAD) == 0:
            relay(TURNS + i // (TILES // LEAD))

    lags(0, TURNS, True, beside)

    @pl.loop(TURNS, STEPS - 1)
    def _(u):
        step(u, 1, u + LEAD < STEPS)

    lags(0, TURNS - 1, False)
    step(STEPS - 1, 1, False)
    lags(TURNS - 1, 1, False)

    half = TILES // 2
    blank = jnp.zeros((1, F2), jnp.float32)
    for ch in range(CH_DEV):
        line = pl.ds(row_me * wide + ch * row_total + col_me * CH_DEV + ch, 1)
        for i in range(TILES):
            for n in range(2):
                acc[i, n, line] = blank

    for k in range(half):
        @pl.loop(0, col_total)
        def _(j):
            line = pl.ds(pl.multiple_of(j * row_total, 16), row_total)
            for n in range(2):
                a, b = acc[k, n, line, :], acc[half + k, n, line, :]
                first = HALF + k * TILE + n * F2
                result[j, :, first : first + F2] = (a + b).astype(jnp.bfloat16)
                down_ref[k, n, line, :] = (a - b).astype(jnp.bfloat16)

    for k in range(half):
        side = jnp.concatenate([down_ref[k, n] for n in range(2)], axis=1)
        turned = dot(side, flip_ref[...]).astype(jnp.bfloat16)
        result[:, :, HALF - (k + 1) * TILE : HALF - k * TILE] = turned.reshape(col_total, row_total, TILE)

    settle(glab.at[pl.ds(1, rows - 1)], a_send.at[PARTS])
    for part in range(PARTS):
        settle(got.at[part, pl.ds(1, rows - 1)], a_send.at[part])
    whole, short = col_all.at[:, 0], col_all.at[pl.ds(0, STEPS - TURNS), 0]
    for d in range(1, hops + 1):
        cut = 1 if d == hops and hops > 1 else 0
        up, down = row_me + d, row_me - d
        pl.when(up <= last - cut)(lambda k=2 * d - 2: settle(whole, z_send.at[k]))
        pl.when(down >= cut)(lambda k=2 * d - 1: settle(whole, z_send.at[k]))
        if cut:
            pl.when(up == last)(lambda k=2 * d - 2: settle(short, z_send.at[k]))
            pl.when(down == 0)(lambda k=2 * d - 1: settle(short, z_send.at[k]))
    for d in range(1, hops):
        sent = (far_up & (row_me + d <= last)) | (far_down & (row_me - d >= 0))
        pl.when(sent)(lambda k=2 * hops + d - 1: settle(whole, z_send.at[k]))
    if hops > 1:
        pl.when(near_up | near_down)(lambda: settle(short, z_send.at[3 * hops - 1]))
    settle(row_all.at[:, pl.ds(0, chips - 1)], x_send.at[0])
    settle(row_all.at[:, 0], x_send.at[1])
    settle(row_all.at[:, pl.ds(0, chips - 1)], x_send.at[2])


def pairs_of(window, file_channels, file_counts):
    rows, cols = lax.axis_size("row"), lax.axis_size("col")
    row_total, col_total = cols * CH_DEV, rows * CH_DEV
    pairs = row_total * col_total
    order = 2 * PSEG * row_total
    block = (QUADS, BLOCK, F2)
    return pl.pallas_call(
        pair_kernel,
        out_shape=jax.ShapeDtypeStruct((col_total, row_total, LAGS), jnp.bfloat16),
        in_specs=[pl.BlockSpec(memory_space=pltpu.VMEM)] + [pl.BlockSpec(memory_space=pltpu.SMEM)] * 2,
        out_specs=pl.BlockSpec(memory_space=pltpu.VMEM),
        scratch_shapes=[
            pltpu.VMEM((2, N1, N2), jnp.float32),
            pltpu.VMEM((2 * N2, 2 * F2), jnp.bfloat16),
            pltpu.VMEM((2 * N2, 2 * F2), jnp.bfloat16),
            pltpu.VMEM((3, N1, F2), jnp.float32),
            pltpu.VMEM((order, order), jnp.bfloat16),
            pltpu.VMEM((TILE, TILE), jnp.bfloat16),
            pltpu.VMEM((PARTS, rows, CAP * PSEG, NT), jnp.bfloat16),
            pltpu.VMEM((rows, CAP * PSEG, 128), jnp.bfloat16),
            pltpu.VMEM((PARTS, rows, CAP * PSEG, NT), jnp.bfloat16),
            pltpu.VMEM((rows, CAP * PSEG, 128), jnp.bfloat16),
            pltpu.VMEM((ROWS, NT), jnp.float32),
            pltpu.VMEM((N1 * ROWS, 2 * N2), jnp.float32),
            pltpu.VMEM((TURNS, TILES, PAIR, TILE), jnp.bfloat16),
            pltpu.VMEM((STEPS, cols) + block, jnp.bfloat16),
            pltpu.VMEM((STEPS, rows) + block, jnp.bfloat16),
            pltpu.VMEM((QUADS, 2 * PSEG, row_total, F2), jnp.bfloat16),
            pltpu.VMEM((QUADS, BLOCK, F2), jnp.float32),
            pltpu.VMEM((TURNS, 2, QUADS, pairs, F2), jnp.bfloat16),
            pltpu.VMEM((TILES, 2, pairs, F2), jnp.float32),
            pltpu.VMEM((TILES // 2, 2, pairs, F2), jnp.bfloat16),
            pltpu.SemaphoreType.DMA((PARTS + 1,)),
            pltpu.SemaphoreType.DMA((PARTS,)),
            pltpu.SemaphoreType.DMA,
            pltpu.SemaphoreType.DMA((3 * (rows // 2),)),
            pltpu.SemaphoreType.DMA((rows, STEPS)),
            pltpu.SemaphoreType.DMA((3,)),
            pltpu.SemaphoreType.DMA((STEPS,)),
            pltpu.SemaphoreType.DMA((STEPS,)),
        ],
        compiler_params=pltpu.CompilerParams(
            vmem_limit_bytes=48 << 20, collective_id=0, has_side_effects=True
        ),
    )(window, file_channels, file_counts)


def local(strain, file_channels, file_counts, window_start):
    window = lax.dynamic_slice_in_dim(strain, window_start[0], SEGS * NT, 1)
    return jnp.transpose(pairs_of(window, file_channels, file_counts), (1, 0, 2))


def solution(mesh):
    placed = (P(("row", "col"), None), P(("row", "col")), P(("row", "col")), P(("row", "col")))
    return jax.shard_map(
        local, mesh=mesh, in_specs=placed, out_specs=P("row", "col", None), check_vma=False
    )
```

```python
import functools
import math

import jax
import jax.numpy as jnp
import numpy as np
from jax import lax
from jax.experimental import pallas as pl
from jax.experimental.pallas import tpu as pltpu
from jax.sharding import PartitionSpec as P

NF = 2048
NT = 4096
LAGS = 1024
SEGS = 8
CH_DEV = 4
CAP = 2
SMOOTH = 32
EDGE = 128
N1 = 16
N2 = NT // N1
F2 = NF // N1
HALF = LAGS // 2
PARTS = 2
PSEG = SEGS // PARTS
ROWS = CH_DEV * PSEG
BLOCK = 2 * ROWS
QUADS = 4
PAIR = QUADS * F2
TURNS = NF // PAIR
STEPS = PARTS * TURNS
TILE = 256
TILES = 2 * HALF // TILE
CORES = 2
LEAD = 2
MESH = pl.DeviceIdType.MESH


def wave(k, period):
    bits = period.bit_length() - 1
    k = k & (period - 1)
    quarter = (4 * k + period // 2) >> bits
    r = (4 * k - (quarter << bits)).astype(jnp.float32) * np.float32(0.5 * np.pi / period)
    r2 = r * r
    odd = r * (1 + r2 * (-1 / 6 + r2 * (1 / 120 + r2 * (-1 / 5040 + r2 * (1 / 362880)))))
    even = 1 + r2 * (-1 / 2 + r2 * (1 / 24 + r2 * (-1 / 720 + r2 * (1 / 40320))))
    swap = (quarter & 1) == 1
    c, s = jnp.where(swap, odd, even), jnp.where(swap, even, odd)
    return jnp.where(((quarter + 1) & 2) == 2, -c, c), jnp.where((quarter & 2) == 2, -s, s)


def grid(shape):
    return [lax.broadcasted_iota(jnp.int32, shape, n) for n in range(2)]


def forward_tables(tw_ref, hi_ref, lo_ref, shape_ref):
    f1, n2 = grid((N1, N2))
    c, s = wave(f1 * n2, NT)
    tw_ref[0], tw_ref[1] = c, -s
    n2, f2 = grid((N2, F2))
    c, s = wave(n2 * f2, N2)
    for block, (r, l) in ((c, (0, 0)), (-s, (0, 1)), (s, (1, 0)), (c, (1, 1))):
        high = block.astype(jnp.bfloat16)
        at = slice(r * N2, (r + 1) * N2), slice(l * F2, (l + 1) * F2)
        hi_ref[at] = high
        lo_ref[at] = (block - high.astype(jnp.float32)).astype(jnp.bfloat16)
    f1, f2 = grid((N1, F2))
    f = f1 + N1 * f2
    c, s = wave(f, 2 * NT)
    rise = wave(jnp.minimum(jnp.minimum(2 * f + 1, 2 * NF - 2 * f - 1), 2 * EDGE), 8 * EDGE)[1]
    shape_ref[0], shape_ref[1], shape_ref[2] = rise * rise, c, -s


def lag_tables(w_ref):
    scale = np.float32(1.0 / math.sqrt(SEGS * NF))
    for k in range(HALF // TILE):
        f2, m = grid((F2, TILE))
        bc, bs = wave(N1 * f2 * (2 * (m + k * TILE) + 1), 2 * NT)
        f1, m = grid((N1, TILE))
        fc, fs = [v * scale for v in wave(f1 * (2 * (m + k * TILE) + 1), 2 * NT)]
        for f in range(N1):
            ac, as_ = fc[f : f + 1], fs[f : f + 1]
            t, at = f * F2 // PAIR, slice(f * F2 % PAIR, f * F2 % PAIR + F2)
            w_ref[t, k, at, :] = (ac * bc - as_ * bs).astype(jnp.bfloat16)
            w_ref[t, HALF // TILE + k, at, :] = (-(as_ * bc + ac * bs)).astype(jnp.bfloat16)


def order_tables(perm_ref, flip_ref, row_total):
    row, lane = grid((perm_ref.shape[0], F2))
    k, g = lax.div(row, row_total), lax.rem(row, row_total)
    c, s = lax.div(k, PSEG), lax.rem(k, PSEG)
    at = lax.div(g, CH_DEV) * BLOCK + c * ROWS + lax.rem(g, CH_DEV) * PSEG + s
    for n in range(perm_ref.shape[1] // F2):
        perm_ref[:, n * F2 : (n + 1) * F2] = jnp.where(at == lane + n * F2, 1.0, 0.0).astype(jnp.bfloat16)
    row, lane = grid((TILE, TILE))
    flip_ref[...] = jnp.where(row + lane == TILE - 1, 1.0, 0.0).astype(jnp.bfloat16)


def shifted(value, lanes, amount):
    rolled = pltpu.roll(value, amount % F2, 1)
    source = lanes - amount
    return jnp.where((source >= 0) & (source < F2), rolled, 0.0)


def greet(axes):
    count = 0
    barrier = pltpu.get_barrier_semaphore()
    for axis in axes:
        size, me = lax.axis_size(axis), lax.axis_index(axis)
        for d in range(1, size):
            pl.semaphore_signal(barrier, inc=1, device_id={axis: lax.rem(me + d, size)}, device_id_type=MESH)
            count += 1
    return lambda: pl.semaphore_wait(barrier, count)


def tree(terms):
    while len(terms) > 1:
        terms = [terms[k] + terms[k + 1] for k in range(0, len(terms), 2)]
    return terms[0]


def combine(values, weights):
    total = None
    for v, w in zip(values, weights):
        if abs(w) < 1e-9:
            continue
        term = v if abs(w - 1) < 1e-9 else (-v if abs(w + 1) < 1e-9 else v * np.float32(w))
        total = term if total is None else total + term
    return total


def dot(a, b):
    return jnp.dot(a, b, preferred_element_type=jnp.float32)


def chosen_rows(label):
    count = label.shape[0]
    row = lax.broadcasted_iota(jnp.int32, label.shape, 0)
    lane = lax.broadcasted_iota(jnp.int32, label.shape, 1)
    hit = (label == (lane // PSEG).astype(jnp.float32)) & (lax.rem(row, PSEG) == lax.rem(lane, PSEG))
    picks = jnp.where(hit, 1.0, 0.0)
    if count < 128:
        picks = jnp.concatenate([picks, jnp.zeros((128 - count, 128), jnp.float32)], axis=0)
    return jnp.transpose(picks)[:ROWS, :count].astype(jnp.bfloat16)


def spectra_part(part, picks, got, x_ref, z_ref, tw_ref, hi_ref, lo_ref, shape_ref, put):
    x_ref[...] = dot(picks, got[part].reshape(-1, NT))
    cosines = np.cos(2 * np.pi * np.arange(N1) / N1)
    sines = np.sin(2 * np.pi * np.arange(N1) / N1)
    for h in range(0, N2, 128):
        xs = [x_ref[:, k * N2 + h : k * N2 + h + 128] for k in range(N1)]
        even = [xs[k] + xs[k + N1 // 2] for k in range(N1 // 2)]
        odd = [xs[k] - xs[k + N1 // 2] for k in range(N1 // 2)]
        for f in range(N1 // 2 + 1):
            src = even if f % 2 == 0 else odd
            re = combine(src, [cosines[f * k % N1] for k in range(N1 // 2)])
            im = combine(src, [-sines[f * k % N1] for k in range(N1 // 2)])
            for f1, sign in {f: 1.0, (N1 - f) % N1: -1.0}.items() if f not in (0, N1 // 2) else ((f, 1.0),):
                tc = tw_ref[0, f1 : f1 + 1, h : h + 128]
                ts = tw_ref[1, f1 : f1 + 1, h : h + 128]
                if im is None:
                    zr, zi = re * tc, re * ts
                else:
                    i = im if sign > 0 else -im
                    zr, zi = re * tc - i * ts, re * ts + i * tc
                z_ref[f1 * ROWS : (f1 + 1) * ROWS, h : h + 128] = zr
                z_ref[f1 * ROWS : (f1 + 1) * ROWS, N2 + h : N2 + h + 128] = zi
    z = z_ref[...]
    zh = z.astype(jnp.bfloat16)
    zl = (z - zh.astype(jnp.float32)).astype(jnp.bfloat16)
    z_ref[:, : 2 * F2] = dot(zh, hi_ref[...]) + dot(zl, hi_ref[...]) + dot(zh, lo_ref[...])
    lanes = lax.broadcasted_iota(jnp.int32, (ROWS, F2), 1)
    piece = lambda f1, c: z_ref[f1 * ROWS : (f1 + 1) * ROWS, c * F2 : (c + 1) * F2]
    power = []
    for f1 in range(N1):
        re, im = piece(f1, 0), piece(f1, 1)
        power.append(re * re + im * im)
    prefix, suffix = [power[0]], [power[-1]]
    for k in range(1, N1):
        prefix.append(prefix[-1] + power[k])
        suffix.append(suffix[-1] + power[N1 - 1 - k])
    suffix = suffix[::-1]
    total = prefix[-1]
    reach = SMOOTH // N1
    middle = total
    for k in range(1, reach):
        middle = middle + shifted(total, lanes, k) + shifted(total, lanes, -k)
    for f1 in range(N1):
        window = middle + shifted(suffix[f1], lanes, reach) + shifted(prefix[f1], lanes, -reach)
        scale = shape_ref[0, f1 : f1 + 1] * lax.rsqrt(window * (1.0 / (2 * SMOOTH + 1)) + 1e-06)
        re, im = piece(f1, 0) * scale, piece(f1, 1) * scale
        tc, ts = shape_ref[1, f1 : f1 + 1], shape_ref[2, f1 : f1 + 1]
        put(part * TURNS + f1 // QUADS, f1 % QUADS, re, im, re * tc - im * ts, re * ts + im * tc)


def route(chan_ref, count_ref, cols, height):
    slots = chan_ref.shape[0]
    row = lax.broadcasted_iota(jnp.int32, (height, 128), 0)
    lane = lax.broadcasted_iota(jnp.int32, (height, 128), 1)
    place = lax.div(row, PSEG)
    owners = [lax.div(chan_ref[s], CH_DEV * cols) for s in range(slots)]
    live = [s < count_ref[0] for s in range(slots)]
    picks = jnp.zeros((height, 128), jnp.float32)
    label = jnp.full((height, 128), -1.0, jnp.float32)
    for s in range(slots):
        position = jnp.int32(0)
        for e in range(s):
            position = position + jnp.where(live[e] & (owners[e] == owners[s]), 1, 0)
        target = jnp.where(live[s], owners[s] * CAP + position, -1)
        hit = place == target
        picks = jnp.where(hit & (lax.rem(lane, slots) == s), 1.0, picks)
        label = jnp.where(hit, lax.rem(chan_ref[s], CH_DEV).astype(jnp.float32), label)
    picks = jnp.where(lax.rem(row, PSEG) == lax.div(lane, slots), picks, 0.0)
    return picks[:, : PSEG * slots].astype(jnp.bfloat16), label.astype(jnp.bfloat16)


def pair_kernel(win_ref, chan_hbm, count_hbm, *refs):
    result, tables, refs = refs[0], refs[1:5], refs[5:]
    perm_ref, flip_ref, refs = refs[0], refs[1], refs[2:]
    out_ref, lab_ref, got, glab, x_ref, z_ref, w_ref, row_all, col_all, v_ref, b32, cross, acc, down_ref = refs[:14]
    a_send, a_recv, lab_recv, z_send, z_recv, x_send, x_same, x_mate, chan_ref, count_ref, fetch_sem = refs[14:]
    rows, cols = lax.axis_size("row"), lax.axis_size("col")
    row_total, col_total = cols * CH_DEV, rows * CH_DEV
    wide = CH_DEV * row_total
    row_me, col_me = lax.axis_index("row"), lax.axis_index("col")
    hops, chips = rows // 2, cols // CORES
    far = lax.rem(row_me + hops, rows)
    chip, core = col_me // CORES, lax.rem(col_me, CORES)
    mate = chip * CORES + (1 - core)
    chip_at = lambda d: lax.rem(chip + chips - d, chips) * CORES

    fetches = [pltpu.make_async_copy(f, t, fetch_sem.at[n]) for n, (f, t) in enumerate(((chan_hbm, chan_ref), (count_hbm, count_ref)))]
    for fetch in fetches:
        fetch.start()
    met = greet(("row", "col"))
    for fetch in fetches:
        fetch.wait()
    routing, label = route(chan_ref, count_ref, cols, rows * CAP * PSEG)
    lab_ref[...] = label.reshape(lab_ref.shape)
    for part in range(PARTS):
        window = [win_ref[:, (part * PSEG + k) * NT : (part * PSEG + k + 1) * NT] for k in range(PSEG)]
        moved = dot(routing, jnp.concatenate(window, axis=0)).astype(jnp.bfloat16)
        out_ref[part] = moved.reshape(out_ref.shape[1:])
    met()

    def remote(src, dst, send, recv, peer):
        return pltpu.make_async_remote_copy(
            src_ref=src, dst_ref=dst, send_sem=send, recv_sem=recv, device_id=peer, device_id_type=MESH
        )

    def settle(ref, sem):
        pltpu.make_async_copy(ref, ref, sem).wait()

    for d in range(1, rows):
        peer = lax.rem(row_me + d, rows)
        remote(lab_ref.at[peer], glab.at[d], a_send.at[PARTS], lab_recv, {"row": peer}).start()
    for part in range(PARTS):
        for d in range(1, rows):
            peer = lax.rem(row_me + d, rows)
            remote(out_ref.at[part, peer], got.at[part, d], a_send.at[part], a_recv.at[part], {"row": peer}).start()
    glab[0] = lab_ref[row_me]
    for part in range(PARTS):
        got[part, 0] = out_ref[part, row_me]

    last = rows - 1
    far_up, far_down = (far < row_me) & (row_me < last), (far > row_me) & (row_me > 0)
    near_up, near_down = row_me == last - 1, row_me == 1
    near = jnp.where(near_up, row_me - (hops - 1), row_me + (hops - 1))

    def z_copy(u, origin, peer, k):
        block = col_all.at[u, origin]
        return remote(block, block, z_send.at[k], z_recv.at[origin, u], {"row": peer})

    def x_copy(u, origin, peer, k):
        sem = x_same if k == 0 else x_mate
        return remote(row_all.at[u, origin], row_all.at[u, origin], x_send.at[k], sem.at[u], {"col": peer})

    def begin(u, part):
        for d in range(hops, 0, -1):
            up, down = row_me + d, row_me - d
            cut = 1 if part == PARTS - 1 and d == hops and hops > 1 else 0
            pl.when(up <= last - cut)(z_copy(u, row_me, up, 2 * d - 2).start)
            pl.when(down >= cut)(z_copy(u, row_me, down, 2 * d - 1).start)
        for d in range(1, chips):
            x_copy(u, col_me, chip_at(d) + core, 0).start()
        x_copy(u, col_me, mate, 1).start()

    def relay(u):
        settled = lambda origin: settle(col_all.at[u, pl.ds(0, 1)], z_recv.at[origin, u])
        if hops > 1:

            @pl.when((u >= TURNS * (PARTS - 1)) & (near_up | near_down))
            def _():
                settled(near)
                pl.when(near_up)(z_copy(u, near, last, 2 * hops + hops - 1).start)
                pl.when(near_down)(z_copy(u, near, 0, 2 * hops + hops - 1).start)

        @pl.when(far_up | far_down)
        def _():
            settled(far)
            for d in range(1, hops):
                k = 2 * hops + d - 1
                pl.when(far_up & (row_me + d <= last))(z_copy(u, far, row_me + d, k).start)
                pl.when(far_down & (row_me - d >= 0))(z_copy(u, far, row_me - d, k).start)

    def forward(u):
        settle(row_all.at[u, pl.ds(0, chips - 1)], x_same.at[u])
        for d in range(1, chips):
            x_copy(u, chip_at(d) + core, mate, 2).start()

    def origin_of(k):
        origin, bit = row_me, 1
        while bit < rows:
            flip = lax.rem(k // bit, 2)
            origin = origin + flip * bit * (1 - 2 * lax.rem(row_me // bit, 2))
            bit *= 2
        return origin

    def arrive(u):
        settle(row_all.at[u, pl.ds(0, chips)], x_mate.at[u])
        for q in range(0, QUADS, 2):
            sides = [row_all[u, :, q + n].reshape(-1, F2) for n in range(2)]
            turned = dot(perm_ref[...], jnp.concatenate(sides, axis=1)).astype(jnp.bfloat16)
            for n in range(2):
                for j in range(2 * PSEG):
                    v_ref[q + n, j] = turned[j * row_total : (j + 1) * row_total, n * F2 : (n + 1) * F2]

    origins = [origin_of(k) for k in range(rows)]
    relays_far, relays_near = far_up | far_down, near_up | near_down

    def meet(u, part, k, more):
        origin = origins[k]
        if k > 0:
            known = (origin == far) & relays_far
            if hops > 1 and part == PARTS - 1:
                known = known | ((origin == near) & relays_near)

            @pl.when(jnp.logical_not(known))
            def _():
                settle(col_all.at[u, pl.ds(0, 1)], z_recv.at[origin, u])

        if k == 1:
            if more is not False:
                pl.when(more)(lambda: relay(u + LEAD))
        if k == 2 % rows:
            if more is not False:
                pl.when(u + LEAD < STEPS)(lambda: forward(u + LEAD))

    def put(u, q, re, im, tr, ti):
        for c, (a, b) in enumerate(((re, tr), (im, ti))):
            at = slice(c * ROWS, (c + 1) * ROWS)
            col_all[u, row_me, q, at] = a.astype(jnp.bfloat16)
            row_all[u, col_me, q, at] = b.astype(jnp.bfloat16)

    def cross_item(u, k):
        origin, now = origins[k], lax.rem(u, TURNS)
        for q in range(QUADS):
            b32[q] = col_all[u, origin, q].astype(jnp.float32)
        for q in range(QUADS):
            for ch in range(CH_DEV):
                spread = lambda r: jnp.broadcast_to(b32[q, r : r + 1, :], (16, F2)).astype(jnp.bfloat16)
                br = [spread(ch * PSEG + s) for s in range(PSEG)]
                bi = [spread(ROWS + ch * PSEG + s) for s in range(PSEG)]
                for g in range(0, row_total, 16):
                    real, imag = [], []
                    for s in range(PSEG):
                        ar, ai = v_ref[q, s, g : g + 16], v_ref[q, PSEG + s, g : g + 16]
                        real.append(br[s] * ar + bi[s] * ai)
                        imag.append(br[s] * ai - bi[s] * ar)
                    line = pl.ds(pl.multiple_of(origin * wide + ch * row_total + g, 16), 16)
                    cross[now, 0, q, line] = tree(real)
                    cross[now, 1, q, line] = tree(imag)

    def lags(first, count, fresh, beside=None):
        for i in range(TILES):
            if beside is not None:
                beside(i)
            side = [cross[first + n, i // (TILES // 2), q] for n in range(count) for q in range(QUADS)]
            table = w_ref[pl.ds(first, count), i].reshape(count * PAIR, TILE)
            term = dot(jnp.concatenate(side, axis=1), table)
            for h in range(2):
                piece = term[:, h * F2 : (h + 1) * F2]
                acc[i, h] = piece if fresh else acc[i, h] + piece

    forward_tables(*tables)
    lag_tables(w_ref)
    order_tables(perm_ref, flip_ref, row_total)
    settle(glab.at[pl.ds(1, rows - 1)], lab_recv)
    settle(got.at[0, pl.ds(1, rows - 1)], a_recv.at[0])
    picks = chosen_rows(glab[...].reshape(-1, 128).astype(jnp.float32))
    spectra_part(0, picks, got, x_ref, z_ref, *tables, put)

    @pl.loop(0, TURNS)
    def _(u):
        begin(u, 0)

    for u in range(LEAD):
        forward(u)
    settle(got.at[1, pl.ds(1, rows - 1)], a_recv.at[1])
    spectra_part(1, picks, got, x_ref, z_ref, *tables, put)

    @pl.loop(TURNS, STEPS)
    def _(u):
        begin(u, 1)

    for u in range(LEAD):
        relay(u)

    def step(u, part, more):
        arrive(u)
        for k in range(rows):
            meet(u, part, k, more)
            cross_item(u, k)

    @pl.loop(0, TURNS)
    def _(u):
        step(u, 0, u + LEAD < TURNS)

    def beside(i):
        if i % (TILES // LEAD) == 0:
            relay(TURNS + i // (TILES // LEAD))

    lags(0, TURNS, True, beside)

    @pl.loop(TURNS, STEPS - 1)
    def _(u):
        step(u, 1, u + LEAD < STEPS)

    lags(0, TURNS - 1, False)
    step(STEPS - 1, 1, False)
    lags(TURNS - 1, 1, False)

    half = TILES // 2
    blank = jnp.zeros((1, F2), jnp.float32)
    for ch in range(CH_DEV):
        line = pl.ds(row_me * wide + ch * row_total + col_me * CH_DEV + ch, 1)
        for i in range(TILES):
            for n in range(2):
                acc[i, n, line] = blank

    for k in range(half):
        @pl.loop(0, col_total)
        def _(j):
            line = pl.ds(pl.multiple_of(j * row_total, 16), row_total)
            for n in range(2):
                a, b = acc[k, n, line, :], acc[half + k, n, line, :]
                first = HALF + k * TILE + n * F2
                result[j, :, first : first + F2] = (a + b).astype(jnp.bfloat16)
                down_ref[k, n, line, :] = (a - b).astype(jnp.bfloat16)

    for k in range(half):
        side = jnp.concatenate([down_ref[k, n] for n in range(2)], axis=1)
        turned = dot(side, flip_ref[...]).astype(jnp.bfloat16)
        result[:, :, HALF - (k + 1) * TILE : HALF - k * TILE] = turned.reshape(col_total, row_total, TILE)

    settle(glab.at[pl.ds(1, rows - 1)], a_send.at[PARTS])
    for part in range(PARTS):
        settle(got.at[part, pl.ds(1, rows - 1)], a_send.at[part])
    whole, short = col_all.at[:, 0], col_all.at[pl.ds(0, STEPS - TURNS), 0]
    for d in range(1, hops + 1):
        cut = 1 if d == hops and hops > 1 else 0
        up, down = row_me + d, row_me - d
        pl.when(up <= last - cut)(lambda k=2 * d - 2: settle(whole, z_send.at[k]))
        pl.when(down >= cut)(lambda k=2 * d - 1: settle(whole, z_send.at[k]))
        if cut:
            pl.when(up == last)(lambda k=2 * d - 2: settle(short, z_send.at[k]))
            pl.when(down == 0)(lambda k=2 * d - 1: settle(short, z_send.at[k]))
    for d in range(1, hops):
        sent = (far_up & (row_me + d <= last)) | (far_down & (row_me - d >= 0))
        pl.when(sent)(lambda k=2 * hops + d - 1: settle(whole, z_send.at[k]))
    if hops > 1:
        pl.when(near_up | near_down)(lambda: settle(short, z_send.at[3 * hops - 1]))
    settle(row_all.at[:, pl.ds(0, chips - 1)], x_send.at[0])
    settle(row_all.at[:, 0], x_send.at[1])
    settle(row_all.at[:, pl.ds(0, chips - 1)], x_send.at[2])


def pairs_of(window, file_channels, file_counts):
    rows, cols = lax.axis_size("row"), lax.axis_size("col")
    row_total, col_total = cols * CH_DEV, rows * CH_DEV
    pairs = row_total * col_total
    order = 2 * PSEG * row_total
    block = (QUADS, BLOCK, F2)
    return pl.pallas_call(
        pair_kernel,
        out_shape=jax.ShapeDtypeStruct((col_total, row_total, LAGS), jnp.bfloat16),
        in_specs=[pl.BlockSpec(memory_space=pltpu.VMEM)] + [pl.BlockSpec(memory_space=pltpu.HBM)] * 2,
        out_specs=pl.BlockSpec(memory_space=pltpu.VMEM),
        scratch_shapes=[
            pltpu.VMEM((2, N1, N2), jnp.float32),
            pltpu.VMEM((2 * N2, 2 * F2), jnp.bfloat16),
            pltpu.VMEM((2 * N2, 2 * F2), jnp.bfloat16),
            pltpu.VMEM((3, N1, F2), jnp.float32),
            pltpu.VMEM((order, order), jnp.bfloat16),
            pltpu.VMEM((TILE, TILE), jnp.bfloat16),
            pltpu.VMEM((PARTS, rows, CAP * PSEG, NT), jnp.bfloat16),
            pltpu.VMEM((rows, CAP * PSEG, 128), jnp.bfloat16),
            pltpu.VMEM((PARTS, rows, CAP * PSEG, NT), jnp.bfloat16),
            pltpu.VMEM((rows, CAP * PSEG, 128), jnp.bfloat16),
            pltpu.VMEM((ROWS, NT), jnp.float32),
            pltpu.VMEM((N1 * ROWS, 2 * N2), jnp.float32),
            pltpu.VMEM((TURNS, TILES, PAIR, TILE), jnp.bfloat16),
            pltpu.VMEM((STEPS, cols) + block, jnp.bfloat16),
            pltpu.VMEM((STEPS, rows) + block, jnp.bfloat16),
            pltpu.VMEM((QUADS, 2 * PSEG, row_total, F2), jnp.bfloat16),
            pltpu.VMEM((QUADS, BLOCK, F2), jnp.float32),
            pltpu.VMEM((TURNS, 2, QUADS, pairs, F2), jnp.bfloat16),
            pltpu.VMEM((TILES, 2, pairs, F2), jnp.float32),
            pltpu.VMEM((TILES // 2, 2, pairs, F2), jnp.bfloat16),
            pltpu.SemaphoreType.DMA((PARTS + 1,)),
            pltpu.SemaphoreType.DMA((PARTS,)),
            pltpu.SemaphoreType.DMA,
            pltpu.SemaphoreType.DMA((3 * (rows // 2),)),
            pltpu.SemaphoreType.DMA((rows, STEPS)),
            pltpu.SemaphoreType.DMA((3,)),
            pltpu.SemaphoreType.DMA((STEPS,)),
            pltpu.SemaphoreType.DMA((STEPS,)),
            pltpu.SMEM(file_channels.shape, jnp.int32),
            pltpu.SMEM(file_counts.shape, jnp.int32),
            pltpu.SemaphoreType.DMA((2,)),
        ],
        compiler_params=pltpu.CompilerParams(
            vmem_limit_bytes=48 << 20, collective_id=0, has_side_effects=True
        ),
    )(window, file_channels, file_counts)


def local(strain, file_channels, file_counts, window_start):
    window = lax.dynamic_slice_in_dim(strain, window_start[0], SEGS * NT, 1)
    return jnp.transpose(pairs_of(window, file_channels, file_counts), (1, 0, 2))


def solution(mesh):
    placed = (P(("row", "col"), None), P(("row", "col")), P(("row", "col")), P(("row", "col")))
    return jax.shard_map(
        local, mesh=mesh, in_specs=placed, out_specs=P("row", "col", None), check_vma=False
    )
```
